32 devices in a mesh: tile: 8 (over z, y), obs: 4 (over x, core).
Axes of the slice: x: 2, y: 2, z: 4, core: 2. Of those that a mesh axis runs over, the one named last changes fastest.
Arguments:
- control: float32 [128, 512, 512], P(None, 'tile', 'obs'), may hold values from -6 to 6
- background: bfloat16 [128, 512, 512], P(None, 'tile', 'obs'), may hold values from -6 to 6
- spread: float32 [512, 512], P('tile', 'obs'), may hold values from 0.03 to 0.24
- obs_holder: int32 [8192, 1], P(('tile', 'obs')), may hold values from 0 to 31; in each aligned block of 256 rows (0 to 255, 256 to 511, ...) at most 24 rows name the same one
- obs_anchor: int32 [8192], P(('tile', 'obs')), may hold values from 0 to 8000
- obs_frac: float32 [2, 8192], P(None, ('tile', 'obs')), may hold values from 0 to 1
- innovation: float32 [8192, 616], P(('tile', 'obs')), may hold values from -6 to 6
- inverse_var: float32 [616], replicated, may hold values from 0.5 to 2
- w_first: bfloat16 [128, 512], replicated, may hold values from -0.5 to 0.5
- b_first: float32 [512], replicated, may hold values from -3 to 3
- w_second: bfloat16 [512, 512], replicated, may hold values from -0.25 to 0.25
- b_second: float32 [512], replicated, may hold values from -3 to 3
- w_third: bfloat16 [512, 616], replicated, may hold values from -0.25 to 0.25
Outputs:
- departures: float32 [8192, 616], P(('tile', 'obs'))
- gradient: float32 [128, 512, 512], P(None, 'tile', 'obs')
The draws below stay inside these ranges and needn't reach their ends.
Inputs may be any that keep to these rules, and one draw needn't show every extreme that they name: `obs_holder`: among the observations of one device (aligned blocks of 256 rows) at most 24 name the same holder.
All inputs are finite; a program needn't handle non-finite values.
Results may differ from the reference program's by a relative error of at most 0.0011.
Values may be sent and summed in bfloat16 or wider, within the bound.
A program may use at most 64 MiB of HBM per device.

```python
import math
import jax
import jax.numpy as jnp
import numpy as np
from jax import lax

LEV = 128
HID = 512
CH = 616
SWEEPS = 2
CX = 64
CY = 128
OBS_DEV = 256
CAP = 24
NX = 512
NY = 512
OBS = 8192
N_OBS = 4
DEVICES = 32


def with_ends(drawn, rng, least, top_value):
    dims = drawn.shape
    index_at = [jax.random.randint(jax.random.fold_in(rng, axis), (), 0, dims[axis]) for axis in range(len(dims))]
    drawn = drawn.at[tuple(index_at)].set(least)
    longest = dims.index(max(dims))
    index_at[longest] = (index_at[longest] + 1) % dims[longest]
    return drawn.at[tuple(index_at)].set(top_value)


def levels(key, extent, pieces, least, top_value):
    def one(dim, parts):
        draws = jax.random.uniform(jax.random.fold_in(jax.random.fold_in(key, 6), dim), (parts,), jnp.float32, least / len(pieces), top_value / len(pieces))
        return jnp.repeat(jnp.exp(draws), extent[dim] // parts).reshape((-1,) + (1,) * (len(extent) - dim - 1))

    factor_of = one(*pieces[0])
    for cut in pieces[1:]:
        factor_of = factor_of * one(*cut)
    return factor_of


def routed_block(rng, own, number, rows, number_of, top, reach, lean):
    ranking = jax.random.permutation(rng, number_of)
    heavy_load, common = shares(number_of, rows * top, reach, lean, True), shares(number_of, rows * top, reach, lean, False)
    places = jnp.arange(number_of)

    def named(sizes, turn):
        used = int((sizes > 0).sum())
        fixed = max(1, used // 4)
        passed = fixed + (places - fixed + turn * (used - fixed)) % max(1, number_of - fixed)
        return jnp.zeros((number_of,), jnp.int32).at[ranking[jnp.where(places < fixed, places, passed)]].set(jnp.asarray(sizes, jnp.int32))

    sizes = jnp.where(number % 4 == 0, named(heavy_load, number // 4), named(common, number - number // 4 - 1))
    mixed = jax.random.permutation(jax.random.fold_in(own, 3), number_of)
    source_of, taker = mixed[0:number_of // 2 * 2:2], mixed[1:number_of // 2 * 2:2]
    room = jnp.minimum(sizes[source_of] - 1, reach - sizes[taker]) // 2
    room = jnp.where((source_of == ranking[0]) | (taker == ranking[0]) | (sizes[taker] == 0), 0, jnp.maximum(room, 0))
    passed = jax.random.randint(jax.random.fold_in(own, 4), (number_of // 2,), 0, 1 << 20) % (room + 1)
    sizes = sizes.at[source_of].add(-passed).at[taker].add(passed)
    items = jnp.searchsorted(jnp.cumsum(sizes), jnp.arange(rows * top), side="right").astype(jnp.int32)
    grid = items.reshape(top, rows).T
    grid = grid[jax.random.permutation(jax.random.fold_in(own, 1), rows)]
    turn = jax.random.randint(jax.random.fold_in(own, 2), (rows, 1), 0, top)
    return jnp.take_along_axis(grid, (jnp.arange(top)[None, :] + turn) % top, axis=1)


def shares(count, total, reach, skew, full):
    loads = [(1 << 20) // math.isqrt(rank ** skew) + 1 for rank in range(1, count + 1)]
    largest = reach if full else min(reach, max(-(-total // count), total * loads[0] // sum(loads)))
    least = 1 if total - largest >= count - 1 else 0
    holding, surplus = [largest] + [least] * (count - 1), total - largest - least * (count - 1)
    while surplus > 0:
        free = [i for i in range(1, count) if holding[i] < largest] or [i for i in range(1, count) if holding[i] < reach]
        mass, left = sum([loads[i] for i in free]), surplus
        for i in free:
            more = min(reach - holding[i], max(1, left * loads[i] // mass), surplus)
            holding[i] = holding[i] + more
            surplus = surplus - more
    return np.array(holding)


def bell_draw(rng, extent, scale, reach, cuts=(), kind=jnp.bfloat16):
    loudness = levels(rng, extent, cuts, -0.22, 0.18) if cuts else 1.0
    entries = jax.random.normal(rng, extent, jnp.float32) * scale * loudness
    return jnp.minimum(jnp.maximum(entries, -reach), reach).astype(kind)


def setup_inputs(seed: int = 0) -> dict:
    keys = jax.random.split(jax.random.key(seed), 14)
    control = bell_draw(keys[0], (LEV, NX, NY), 1.0, 6.0, ((1, 8), (2, 4)), jnp.float32)
    background = bell_draw(keys[1], (LEV, NX, NY), 1.0, 6.0, ((1, 8), (2, 4)))
    spread = jnp.clip(jnp.exp(math.log(0.24) - 2.0794415 * jax.random.uniform(keys[2], (NX, NY), jnp.float32) ** levels(keys[2], (NX, NY), ((0, 8), (1, 4)), -0.2, 0.2)), 0.03, 0.24)
    obs_holder_keys = jax.random.split(jax.random.fold_in(keys[3], 1), OBS // OBS_DEV)
    obs_holder_turns = jax.random.permutation(jax.random.fold_in(keys[3], 3), OBS // OBS_DEV)
    obs_holder = jax.vmap(lambda own, number: routed_block(jax.random.fold_in(keys[3], 2), own, number, OBS_DEV, DEVICES, 1, CAP, 2))(obs_holder_keys, obs_holder_turns).reshape((OBS, 1))
    obs_anchor = with_ends(jax.random.randint(keys[4], (OBS,), 0, (CX - 1) * (CY - 1)), jax.random.fold_in(keys[4], 1), 0, ((CX - 1) * (CY - 1)) - 1).astype(jnp.int32)
    obs_frac = jnp.clip(1.0 * jax.random.uniform(keys[5], (2, OBS), jnp.float32) ** levels(keys[5], (2, OBS), ((1, 32),), -0.2, 0.2), 0.0, 1.0)
    innovation = bell_draw(keys[6], (OBS, CH), 1.0, 6.0, ((0, 32),), jnp.float32)
    inverse_var = jnp.clip(jnp.exp(jax.random.uniform(keys[7], (CH,), jnp.float32, math.log(0.5), math.log(2.0))), 0.5, 2.0)
    w_first = bell_draw(keys[8], (LEV, HID), LEV ** -0.5, 0.5)
    b_first = bell_draw(keys[9], (HID,), 1.0, 3.0, (), jnp.float32)
    w_second = bell_draw(keys[10], (HID, HID), HID ** -0.5, 0.25)
    b_second = bell_draw(keys[11], (HID,), 1.0, 3.0, (), jnp.float32)
    w_third = bell_draw(keys[12], (HID, CH), HID ** -0.5, 0.25)
    return {"control": control, "background": background, "spread": spread, "obs_holder": obs_holder, "obs_anchor": obs_anchor, "obs_frac": obs_frac, "innovation": innovation, "inverse_var": inverse_var, "w_first": w_first, "b_first": b_first, "w_second": w_second, "b_second": b_second, "w_third": w_third}


def laplace(field):
    total = jnp.roll(field, -1, 1) + jnp.roll(field, 1, 1)
    total = total + jnp.roll(field, -1, 2) + jnp.roll(field, 1, 2)
    return total - 4.0 * field


def radiances(base, delta, innov, inverse_var, w_first, b_first, w_second, b_second, w_third):
    h_one = jnp.tanh(jnp.dot(base, w_first, preferred_element_type=jnp.float32) + b_first)
    d_one = 1.0 - h_one * h_one
    h_two = jnp.tanh(jnp.dot(h_one.astype(jnp.bfloat16), w_second, preferred_element_type=jnp.float32) + b_second)
    d_two = 1.0 - h_two * h_two
    t_one = (d_one * jnp.dot(delta, w_first, preferred_element_type=jnp.float32)).astype(jnp.bfloat16)
    t_two = (d_two * jnp.dot(t_one, w_second, preferred_element_type=jnp.float32)).astype(jnp.bfloat16)
    change = jnp.dot(t_two, w_third, preferred_element_type=jnp.float32)
    departures = (change - innov) * inverse_var
    s_two = (d_two * jnp.dot(departures.astype(jnp.bfloat16), w_third.T, preferred_element_type=jnp.float32)).astype(jnp.bfloat16)
    s_one = (d_one * jnp.dot(s_two, w_second.T, preferred_element_type=jnp.float32)).astype(jnp.bfloat16)
    return departures, jnp.dot(s_one, w_first.T, preferred_element_type=jnp.float32)


def reference(control, background, spread, obs_holder, obs_anchor, obs_frac, innovation, inverse_var, w_first, b_first, w_second, b_second, w_third):
    increment = control
    for step in range(SWEEPS):
        increment = increment + spread[None] * laplace(increment)
    inc_cols = increment.astype(jnp.bfloat16).reshape(LEV, NX * NY).T
    bg_cols = background.reshape(LEV, NX * NY).T
    holder = obs_holder[:, 0].astype(jnp.int32)
    anchor = obs_anchor.astype(jnp.int32)
    ix = (holder // N_OBS) * CX + anchor // (CY - 1)
    iy = (holder % N_OBS) * CY + anchor % (CY - 1)
    corner = (ix * NY + iy).astype(jnp.int32)
    sources = [corner, corner + NY, corner + 1, corner + NY + 1]
    frac_x = obs_frac[0]
    frac_y = obs_frac[1]
    weights = [(1.0 - frac_x) * (1.0 - frac_y), frac_x * (1.0 - frac_y), (1.0 - frac_x) * frac_y, frac_x * frac_y]
    base = sum(weights[j][:, None] * bg_cols[sources[j]].astype(jnp.float32) for j in range(4)).astype(jnp.bfloat16)
    delta = sum(weights[j][:, None] * inc_cols[sources[j]].astype(jnp.float32) for j in range(4)).astype(jnp.bfloat16)
    blocks = OBS // OBS_DEV

    def one_block(items):
        return radiances(items[0], items[1], items[2], inverse_var, w_first, b_first, w_second, b_second, w_third)

    departures, profile_grad = lax.map(one_block, (base.reshape(blocks, OBS_DEV, LEV), delta.reshape(blocks, OBS_DEV, LEV), innovation.reshape(blocks, OBS_DEV, CH)))
    departures = departures.reshape(OBS, CH)
    profile_grad = profile_grad.reshape(OBS, LEV)
    gathered = jnp.zeros((NX * NY, LEV), jnp.float32)
    for j in range(4):
        gathered = gathered.at[sources[j]].add(weights[j][:, None] * profile_grad)
    adjoint = gathered.T.reshape(LEV, NX, NY)
    for step in range(SWEEPS):
        adjoint = adjoint + laplace(spread[None] * adjoint)
    return departures, control + adjoint
```

```python
import functools

import jax
import jax.numpy as jnp
from jax import lax
from jax.experimental import pallas as pl
from jax.experimental.pallas import tpu as pltpu
from jax.sharding import PartitionSpec as P

SWEEPS = 2
LANES = 128
MESH_ID = pl.DeviceIdType.MESH
F32 = jnp.float32
BF16 = jnp.bfloat16


def vmem(count):
    return [pl.BlockSpec(memory_space=pltpu.VMEM)] * count


def split_two(value):
    high = value.astype(BF16)
    return high, (value - high.astype(F32)).astype(BF16)


def request_kernel(cap, per_row, holder_ref, anchor_ref, frac_ref, req_ref, pos_ref):
    owners = req_ref.shape[0]
    count = holder_ref.shape[0]
    holder = holder_ref[...]
    marks = holder == lax.broadcasted_iota(jnp.int32, (count, owners), 1)
    marks = marks.astype(F32)
    tri = lax.broadcasted_iota(jnp.int32, (count, count), 0) > lax.broadcasted_iota(
        jnp.int32, (count, count), 1
    )
    before = jnp.dot(
        tri.astype(F32).astype(BF16), marks.astype(BF16), preferred_element_type=F32
    )
    rank = jnp.sum(before * marks, axis=1, keepdims=True).astype(jnp.int32)
    pos_ref[...] = holder * cap + rank
    slot = holder * LANES + rank
    anchor = anchor_ref[...].astype(F32)
    ax = jnp.floor((anchor + 0.5) / per_row)
    ay = anchor - ax * per_row
    rows = [ax, ay]
    for axis in range(2):
        value = frac_ref[pl.ds(axis, 1), :]
        for _ in range(3):
            part = value.astype(BF16).astype(F32)
            rows.append(part)
            value = value - part
    index = lax.broadcasted_iota(jnp.int32, (8, count), 0)
    fields = jnp.zeros((8, count), F32)
    for k, row in enumerate(rows):
        fields = jnp.where(index == k, jnp.broadcast_to(row, (8, count)), fields)
    fields = fields.astype(BF16)
    step = 8
    for first in range(0, owners, step):
        lane = lax.broadcasted_iota(jnp.int32, (count, step * LANES), 1) + first * LANES
        chosen = (slot == lane).astype(F32).astype(BF16)
        got = jnp.dot(fields, chosen, preferred_element_type=F32)
        for k in range(step):
            req_ref[first + k] = got[:, k * LANES : (k + 1) * LANES]


def halo_copies(n_tile, n_obs, k, refs, send_sem, recv_sem):
    rows_ref, strips_ref, rows_out, strips_out, corners_out = refs
    tile, obs = lax.axis_index("tile"), lax.axis_index("obs")
    up, down = lax.rem(tile + n_tile - 1, n_tile), lax.rem(tile + 1, n_tile)
    west, east = lax.rem(obs + n_obs - 1, n_obs), lax.rem(obs + 1, n_obs)
    length = strips_ref.shape[1]
    top, end = pl.ds(0, 8), pl.ds(length - 8, 8)
    west_set, east_set = pl.ds(0, 2 * k), pl.ds(2 * k, 2 * k)
    west_edge, east_edge = pl.ds(0, k), pl.ds(2 * k, k)
    plan = [
        (rows_ref.at[pl.ds(0, 2)], rows_out.at[pl.ds(0, 2)], (up, obs)),
        (rows_ref.at[pl.ds(2, 2)], rows_out.at[pl.ds(2, 2)], (down, obs)),
        (strips_ref.at[west_set], strips_out.at[west_set], (tile, west)),
        (strips_ref.at[east_set], strips_out.at[east_set], (tile, east)),
        (strips_ref.at[west_edge, top], corners_out.at[0], (up, west)),
        (strips_ref.at[west_edge, end], corners_out.at[1], (down, west)),
        (strips_ref.at[east_edge, top], corners_out.at[2], (up, east)),
        (strips_ref.at[east_edge, end], corners_out.at[3], (down, east)),
    ]
    peers = [target for _, _, target in plan]
    copies = [
        pltpu.make_async_remote_copy(
            src_ref=source,
            dst_ref=target,
            send_sem=send_sem.at[i],
            recv_sem=recv_sem.at[i],
            device_id=peer,
            device_id_type=MESH_ID,
        )
        for i, (source, target, peer) in enumerate(plan)
    ]
    return peers, copies


def halo_kernel(n_tile, n_obs, k, rows_ref, strips_ref, rows_out, strips_out, corners_out, send_sem, recv_sem):
    peers, copies = halo_copies(
        n_tile, n_obs, k, (rows_ref, strips_ref, rows_out, strips_out, corners_out), send_sem, recv_sem
    )
    barrier = pltpu.get_barrier_semaphore()
    for peer in peers:
        pl.semaphore_signal(barrier, inc=1, device_id=peer, device_id_type=MESH_ID)
    pl.semaphore_wait(barrier, len(peers))
    for copy in copies:
        copy.start()
    for copy in copies:
        copy.wait()


def halo(rows, strips, n_tile, n_obs, k, ident):
    length = strips.shape[2]
    return pl.pallas_call(
        functools.partial(halo_kernel, n_tile, n_obs, k),
        out_shape=(
            jax.ShapeDtypeStruct(rows.shape, rows.dtype),
            jax.ShapeDtypeStruct(strips.shape, strips.dtype),
            jax.ShapeDtypeStruct((4, k, 8, length), strips.dtype),
        ),
        in_specs=vmem(2),
        out_specs=vmem(3),
        scratch_shapes=[pltpu.SemaphoreType.DMA((8,)), pltpu.SemaphoreType.DMA((8,))],
        compiler_params=pltpu.CompilerParams(collective_id=ident, has_side_effects=True),
        name="halo",
    )(rows, strips)


def swap_kernel(n_tile, n_obs, x_ref, out_ref, send_sem, recv_sem, own_sem):
    n = n_tile * n_obs
    me = lax.axis_index("tile") * n_obs + lax.axis_index("obs")

    def spot(k):
        peer = lax.rem(me + k, n)
        return peer, (peer // n_obs, lax.rem(peer, n_obs))

    barrier = pltpu.get_barrier_semaphore()

    def greet(k, _):
        pl.semaphore_signal(barrier, inc=1, device_id=spot(k)[1], device_id_type=MESH_ID)
        return 0

    lax.fori_loop(1, n, greet, 0)
    own = pltpu.make_async_copy(x_ref.at[me], out_ref.at[me], own_sem)
    own.start()
    pl.semaphore_wait(barrier, n - 1)

    def transfer(k):
        peer, place = spot(k)
        return pltpu.make_async_remote_copy(
            src_ref=x_ref.at[peer],
            dst_ref=out_ref.at[me],
            send_sem=send_sem.at[k],
            recv_sem=recv_sem.at[k],
            device_id=place,
            device_id_type=MESH_ID,
        )

    def begin(k, _):
        transfer(k).start()
        return 0

    def finish(k, _):
        transfer(k).wait()
        return 0

    lax.fori_loop(1, n, begin, 0)
    lax.fori_loop(1, n, finish, 0)
    own.wait()


def swap(x, n_tile, n_obs, ident):
    n = n_tile * n_obs
    return pl.pallas_call(
        functools.partial(swap_kernel, n_tile, n_obs),
        out_shape=jax.ShapeDtypeStruct(x.shape, x.dtype),
        in_specs=vmem(1),
        out_specs=pl.BlockSpec(memory_space=pltpu.VMEM),
        scratch_shapes=[
            pltpu.SemaphoreType.DMA((n,)),
            pltpu.SemaphoreType.DMA((n,)),
            pltpu.SemaphoreType.DMA,
        ],
        compiler_params=pltpu.CompilerParams(collective_id=ident, has_side_effects=True),
        name="swap",
    )(x)


def weight_fields(req, rows_x, rows_y):
    slots = req.shape[1]
    ax, ay = req[0:1].astype(jnp.int32), req[1:2].astype(jnp.int32)
    fx = req[2:3] + req[3:4] + req[4:5]
    fy = req[5:6] + req[6:7] + req[7:8]

    def ramp(size, place, frac):
        index = lax.broadcasted_iota(jnp.int32, (size, slots), 0)
        return jnp.where(index == place, 1.0 - frac, jnp.where(index == place + 1, frac, 0.0))

    return ramp(rows_x, ax, fx), ramp(rows_y, ay, fy)


def compact_kernel(cap, req_ref, out_ref):
    owners = req_ref.shape[0]
    out_ref[...] = jnp.concatenate([req_ref[p][:, :cap] for p in range(owners)], axis=1)


def around(value, axis):
    size = value.shape[axis]
    return pltpu.roll(value, 1, axis) + pltpu.roll(value, size - 1, axis)


def strip_setup(k, adjoint, own_ref, strips_ref, corners_ref, dstrips, edge_ref):
    length, levels = own_ref.shape[1], own_ref.shape[2]
    index = lax.broadcasted_iota(jnp.int32, (8, levels), 0)
    strips_d, corners_d, own_d = dstrips

    def extended(base, low, high):
        return jnp.concatenate([base, jnp.where(index < 4, low, high)], axis=0)

    def plain(base):
        return jnp.concatenate([base, jnp.zeros((8, levels), F32)], axis=0)

    for side, (near, far, own, corner_low, corner_high) in enumerate(
        ((2, 3, 0, 2, 3), (0, 1, 1, 0, 1))
    ):
        s_near = extended(strips_ref[near * k], corners_ref[corner_low, 0], corners_ref[corner_high, 0])
        s_far, s_own = plain(strips_ref[far * k]), plain(own_ref[own])
        d_near = extended(strips_d[near * 2 + 1], corners_d[corner_low, 1], corners_d[corner_high, 1])
        if adjoint:
            d_far, d_own = plain(strips_d[far * 2 + 1]), plain(own_d[own])
            h_near = d_near * s_near
            first = s_near + around(h_near, 0) + d_far * s_far + d_own * s_own - 4.0 * h_near
            edge_ref[side] = h_near
            edge_ref[2 + side] = d_near * first
        else:
            first = s_near + d_near * (around(s_near, 0) + s_far + s_own - 4.0 * s_near)
            edge_ref[side] = s_near
            edge_ref[2 + side] = first


def extend_rows(block, rows_ref, level):
    index = lax.broadcasted_iota(jnp.int32, (8, block.shape[1]), 0)
    tile = jnp.zeros((8, block.shape[1]), F32)
    for k, place in enumerate((0, 1, 6, 7)):
        row = rows_ref[k, pl.ds(level, 1), :]
        tile = jnp.where(index == place, jnp.broadcast_to(row, tile.shape), tile)
    return jnp.concatenate([block, tile], axis=0)


def laplace(value, edge_ref, sweep, level):
    size = value.shape[1]
    lane = lax.broadcasted_iota(jnp.int32, value.shape, 1)
    west = pltpu.roll(edge_ref[2 * sweep], lax.rem(size - level, size), 1)
    east = pltpu.roll(edge_ref[2 * sweep + 1], size - 1 - level, 1)
    left = jnp.where(lane == 0, west, pltpu.roll(value, 1, 1))
    right = jnp.where(lane == size - 1, east, pltpu.roll(value, size - 1, 1))
    return around(value, 0) + left + right - 4.0 * value


def sweeps(adjoint, value, spread, edge_ref, level):
    for sweep in range(SWEEPS):
        if adjoint:
            value = value + laplace(spread * value, edge_ref, sweep, level)
        else:
            value = value + spread * laplace(value, edge_ref, sweep, level)
    return value


CHUNK = 8


def gather_level(block, y_ref, x_ref, out_ref, first):
    rows_x = x_ref.shape[0]
    got = jnp.dot(
        jnp.concatenate([block, block], axis=1), y_ref[...], preferred_element_type=F32
    )
    xs = x_ref[...]
    parts = [
        jnp.sum(got[i * rows_x : (i + 1) * rows_x] * xs, axis=0, keepdims=True)
        for i in range(CHUNK)
    ]
    out_ref[pl.ds(first, CHUNK), :] = jnp.concatenate(parts, axis=0)


def gather_kernel(
    control_ref, bg_ref, rows_ref, own_ref, strips_ref, corners_ref, own_d_ref, spread_ref, req_ref,
    base_ref, delta_ref, x_ref, y_ref, d_ref, edge_ref, base_t, delta_t, inc_ref,
):
    step = pl.program_id(0)
    rows_x, rows_y = spread_ref.shape

    @pl.when(step == 0)
    def _():
        xs, ys = weight_fields(req_ref[...], rows_x, rows_y)
        x_ref[...] = xs
        high, low = split_two(ys)
        y_ref[pl.ds(0, rows_y), :] = high
        y_ref[pl.ds(rows_y, rows_y), :] = low
        d_ref[...] = extend_rows(spread_ref[...], rows_ref, rows_ref.shape[1] - 8)
        strip_setup(2, False, own_ref, strips_ref, corners_ref, (strips_ref, corners_ref, own_d_ref), edge_ref)

    spread = d_ref[...]
    for i in range(CHUNK):
        level = step * CHUNK + i
        value = extend_rows(control_ref[i], rows_ref, level)
        value = sweeps(False, value, spread, edge_ref, level)
        inc_ref[pl.ds(i * rows_x, rows_x), :] = value[:rows_x].astype(BF16)
    first = pl.multiple_of(step * CHUNK, CHUNK)
    gather_level(bg_ref[...].reshape(CHUNK * rows_x, rows_y), y_ref, x_ref, base_t, first)
    gather_level(inc_ref[...], y_ref, x_ref, delta_t, first)

    @pl.when(step == pl.num_programs(0) - 1)
    def _():
        base_ref[...] = base_t[...].T.astype(BF16)
        delta_ref[...] = delta_t[...].T.astype(BF16)


def radiance_kernel(
    cap, pos_ref, got_ref, innov_ref, var_ref, w1_ref, b1_ref, w2_ref, b2_ref, w3_ref, dep_ref, out_ref,
):
    count = pos_ref.shape[0]
    both = got_ref.shape[0]
    pos = pos_ref[...]
    peer = jnp.floor((pos.astype(F32) + 0.5) / cap).astype(jnp.int32)
    place = pos + peer * cap
    lane = lax.broadcasted_iota(jnp.int32, (count, both), 1)
    got = got_ref[...]
    pick_b = (lane == place).astype(F32).astype(BF16)
    pick_d = (lane == place + cap).astype(F32).astype(BF16)
    base = jnp.dot(pick_b, got, preferred_element_type=F32).astype(BF16)
    delta = jnp.dot(pick_d, got, preferred_element_type=F32).astype(BF16)

    def forward(a, b):
        return jnp.dot(a, b, preferred_element_type=F32)

    def backward(a, b):
        return lax.dot_general(a, b, (((1,), (1,)), ((), ())), preferred_element_type=F32)

    w1, w2, w3 = w1_ref[...], w2_ref[...], w3_ref[...]
    h_one = jnp.tanh(forward(base, w1) + b1_ref[...])
    d_one = 1.0 - h_one * h_one
    h_two = jnp.tanh(forward(h_one.astype(BF16), w2) + b2_ref[...])
    d_two = 1.0 - h_two * h_two
    t_one = (d_one * forward(delta, w1)).astype(BF16)
    t_two = (d_two * forward(t_one, w2)).astype(BF16)
    dep = (forward(t_two, w3) - innov_ref[...]) * var_ref[...]
    dep_ref[...] = dep
    s_two = (d_two * backward(dep.astype(BF16), w3)).astype(BF16)
    s_one = (d_one * backward(s_two, w2)).astype(BF16)
    grad = backward(s_one, w1).astype(BF16)
    slots = out_ref.shape[0]
    spot = lax.broadcasted_iota(jnp.int32, (count, slots), 1)
    pick = (spot == pos).astype(F32).astype(BF16)
    out_ref[...] = lax.dot_general(
        pick, grad, (((0,), (0,)), ((), ())), preferred_element_type=F32
    ).astype(BF16)


def rim_kernel(rows_x, rows_y, grad_ref, req_ref, rows_ref, strips_ref, grad_t_ref):
    xs, ys = weight_fields(req_ref[...], rows_x, rows_y)
    grad = grad_ref[...]
    grad_t = grad.astype(F32).T
    grad_t_ref[...] = grad_t
    grad_tb = grad_t.astype(BF16)
    for k, y in enumerate((0, 1, rows_y - 1, rows_y - 2)):
        high, low = split_two(xs * ys[y : y + 1])
        strips_ref[k] = jnp.dot(high, grad, preferred_element_type=F32) + jnp.dot(
            low, grad, preferred_element_type=F32
        )
    for k, x in enumerate((0, 1, rows_x - 2, rows_x - 1)):
        high, low = split_two(ys * xs[x : x + 1])
        contract = (((1,), (1,)), ((), ()))
        rows_ref[k] = lax.dot_general(
            grad_tb, high, contract, preferred_element_type=F32
        ) + lax.dot_general(grad_tb, low, contract, preferred_element_type=F32)


def adjoint_kernel(
    control_ref, grad_t_ref, req_ref, rows_ref, own_ref, strips_ref, corners_ref,
    rows_c_ref, strips_c_ref, corners_c_ref, own_d_ref, spread_ref,
    out_ref, x_ref, y_ref, d_ref, edge_ref, lhs_ref,
):
    step = pl.program_id(0)
    rows_x, rows_y = spread_ref.shape

    @pl.when(step == 0)
    def _():
        xs, ys = weight_fields(req_ref[...], rows_x, rows_y)
        x_ref[...] = xs
        high, low = split_two(ys.T)
        y_ref[:, pl.ds(0, rows_y)] = high
        y_ref[:, pl.ds(rows_y, rows_y)] = low
        d_ref[...] = extend_rows(spread_ref[...], rows_c_ref, rows_c_ref.shape[1] - 8)
        strip_setup(1, True, own_ref, strips_ref, corners_ref, (strips_c_ref, corners_c_ref, own_d_ref), edge_ref)

    xs = x_ref[...]
    for i in range(CHUNK):
        row = grad_t_ref[pl.ds(i, 1), :]
        lhs_ref[pl.ds(i * rows_x, rows_x), :] = (xs * row).astype(BF16)
    both = jnp.dot(lhs_ref[...], y_ref[...], preferred_element_type=F32)
    field = both[:, :rows_y] + both[:, rows_y:]
    spread = d_ref[...]
    for i in range(CHUNK):
        level = step * CHUNK + i
        value = extend_rows(field[i * rows_x : (i + 1) * rows_x], rows_ref, level)
        value = sweeps(True, value, spread, edge_ref, level)
        out_ref[i] = control_ref[i] + value[:rows_x]


def whole(array):
    rank = len(array.shape)
    return pl.BlockSpec(array.shape, lambda i: (0,) * rank, pipeline_mode=pl.Buffered(1))


def per_device(
    n_tile, n_obs, control, background, spread, obs_holder, obs_anchor, obs_frac, innovation,
    inverse_var, w_first, b_first, w_second, b_second, w_third,
):
    levels, rows_x, rows_y = control.shape
    owners = n_tile * n_obs
    count = obs_anchor.shape[0]
    channels = innovation.shape[1]
    cap = 3 * count // owners
    slots = owners * cap

    req, pos = pl.pallas_call(
        functools.partial(request_kernel, cap, rows_y - 1),
        out_shape=(
            jax.ShapeDtypeStruct((owners, 8, LANES), F32),
            jax.ShapeDtypeStruct((count, 1), jnp.int32),
        ),
        name="requests",
    )(obs_holder, obs_anchor.reshape(1, count), obs_frac)
    req = swap(req, n_tile, n_obs, 0)
    req = pl.pallas_call(
        functools.partial(compact_kernel, cap),
        out_shape=jax.ShapeDtypeStruct((8, slots), F32),
        name="compact",
    )(req)

    picks_x = (0, 1, rows_x - 2, rows_x - 1)
    rows = jnp.stack([control[:, x, :] for x in picks_x])
    rows_d = jnp.stack([spread[x] for x in picks_x])
    rows = jnp.concatenate([rows, jnp.broadcast_to(rows_d[:, None], (4, 8, rows_y))], axis=1)
    strips = []
    for y in (0, 1, rows_y - 1, rows_y - 2):
        strips.append(control[:, :, y].T)
        strips.append(jnp.broadcast_to(spread[:, y, None], (rows_x, levels)))
    own_c = jnp.stack([strips[0], strips[4]])
    own_d = jnp.stack([strips[1], strips[5]])
    rows_c, strips_c, corners_c = halo(rows, jnp.stack(strips), n_tile, n_obs, 2, 1)

    steps = levels // CHUNK
    block = pl.BlockSpec((CHUNK, rows_x, rows_y), lambda i: (i, 0, 0))
    column = jax.ShapeDtypeStruct((slots, levels), BF16)
    held = [rows_c, own_c, strips_c, corners_c, own_d, spread, req]
    base, delta = pl.pallas_call(
        gather_kernel,
        grid=(steps,),
        out_shape=(column, column),
        in_specs=[block, block] + [whole(a) for a in held],
        out_specs=(whole(column), whole(column)),
        scratch_shapes=[
            pltpu.VMEM((rows_x, slots), F32),
            pltpu.VMEM((2 * rows_y, slots), BF16),
            pltpu.VMEM((rows_x + 8, rows_y), F32),
            pltpu.VMEM((4, rows_x + 8, levels), F32),
            pltpu.VMEM((levels, slots), F32),
            pltpu.VMEM((levels, slots), F32),
            pltpu.VMEM((CHUNK * rows_x, rows_y), BF16),
        ],
        name="gather",
    )(control, background, *held)

    sent = jnp.concatenate(
        [base.reshape(owners, cap, levels), delta.reshape(owners, cap, levels)], axis=1
    )
    got = swap(sent, n_tile, n_obs, 2).reshape(2 * slots, levels)

    departures, grad = pl.pallas_call(
        functools.partial(radiance_kernel, cap),
        out_shape=(
            jax.ShapeDtypeStruct((count, channels), F32),
            jax.ShapeDtypeStruct((slots, levels), BF16),
        ),
        name="radiances",
    )(
        pos, got, innovation, inverse_var.reshape(1, -1), w_first, b_first.reshape(1, -1),
        w_second, b_second.reshape(1, -1), w_third,
    )
    grad = swap(grad.reshape(owners, cap, levels), n_tile, n_obs, 3).reshape(slots, levels)

    rows_a, strips_a, grad_t = pl.pallas_call(
        functools.partial(rim_kernel, rows_x, rows_y),
        out_shape=(
            jax.ShapeDtypeStruct((4, levels, rows_y), F32),
            jax.ShapeDtypeStruct((4, rows_x, levels), F32),
            jax.ShapeDtypeStruct((levels, slots), F32),
        ),
        name="rims",
    )(grad, req)
    own_a = jnp.stack([strips_a[0], strips_a[2]])
    rows_a, strips_a, corners_a = halo(rows_a, strips_a, n_tile, n_obs, 1, 4)

    held = [req, rows_a, own_a, strips_a, corners_a, rows_c, strips_c, corners_c, own_d, spread]
    gradient = pl.pallas_call(
        adjoint_kernel,
        grid=(steps,),
        out_shape=jax.ShapeDtypeStruct(control.shape, F32),
        in_specs=[block, pl.BlockSpec((CHUNK, slots), lambda i: (i, 0))] + [whole(a) for a in held],
        out_specs=block,
        scratch_shapes=[
            pltpu.VMEM((rows_x, slots), F32),
            pltpu.VMEM((slots, 2 * rows_y), BF16),
            pltpu.VMEM((rows_x + 8, rows_y), F32),
            pltpu.VMEM((4, rows_x + 8, levels), F32),
            pltpu.VMEM((CHUNK * rows_x, slots), BF16),
        ],
        name="adjoint",
    )(control, grad_t, *held)
    return (departures, gradient)


def solution(mesh):
    n_tile, n_obs = mesh.shape["tile"], mesh.shape["obs"]
    return jax.shard_map(
        functools.partial(per_device, n_tile, n_obs),
        mesh=mesh,
        in_specs=(
            P(None, "tile", "obs"),
            P(None, "tile", "obs"),
            P("tile", "obs"),
            P(("tile", "obs"), None),
            P(("tile", "obs")),
            P(None, ("tile", "obs")),
            P(("tile", "obs"), None),
            P(),
            P(),
            P(),
            P(),
            P(),
            P(),
        ),
        out_specs=(P(("tile", "obs"), None), P(None, "tile", "obs")),
        check_vma=False,
    )
```

```python
import functools

import jax
import jax.numpy as jnp
from jax import lax
from jax.experimental import pallas as pl
from jax.experimental.pallas import tpu as pltpu
from jax.sharding import PartitionSpec as P

SWEEPS = 2
LANES = 128
MESH_ID = pl.DeviceIdType.MESH
F32 = jnp.float32
BF16 = jnp.bfloat16


def vmem(count):
    return [pl.BlockSpec(memory_space=pltpu.VMEM)] * count


def split_two(value):
    high = value.astype(BF16)
    return high, (value - high.astype(F32)).astype(BF16)


def request_kernel(cap, per_row, holder_ref, anchor_ref, frac_ref, req_ref, pos_ref):
    owners = req_ref.shape[0]
    count = holder_ref.shape[0]
    holder = holder_ref[...]
    marks = holder == lax.broadcasted_iota(jnp.int32, (count, owners), 1)
    marks = marks.astype(F32)
    tri = lax.broadcasted_iota(jnp.int32, (count, count), 0) > lax.broadcasted_iota(
        jnp.int32, (count, count), 1
    )
    before = jnp.dot(
        tri.astype(F32).astype(BF16), marks.astype(BF16), preferred_element_type=F32
    )
    rank = jnp.sum(before * marks, axis=1, keepdims=True).astype(jnp.int32)
    pos_ref[...] = holder * cap + rank
    slot = holder * LANES + rank
    anchor = anchor_ref[...].astype(F32)
    ax = jnp.floor((anchor + 0.5) / per_row)
    ay = anchor - ax * per_row
    rows = [ax, ay]
    for axis in range(2):
        value = frac_ref[pl.ds(axis, 1), :]
        for _ in range(3):
            part = value.astype(BF16).astype(F32)
            rows.append(part)
            value = value - part
    index = lax.broadcasted_iota(jnp.int32, (8, count), 0)
    fields = jnp.zeros((8, count), F32)
    for k, row in enumerate(rows):
        fields = jnp.where(index == k, jnp.broadcast_to(row, (8, count)), fields)
    fields = fields.astype(BF16)
    step = 8
    for first in range(0, owners, step):
        lane = lax.broadcasted_iota(jnp.int32, (count, step * LANES), 1) + first * LANES
        chosen = (slot == lane).astype(F32).astype(BF16)
        got = jnp.dot(fields, chosen, preferred_element_type=F32)
        for k in range(step):
            req_ref[first + k] = got[:, k * LANES : (k + 1) * LANES]


def remote(source, target, send, recv, place):
    return pltpu.make_async_remote_copy(
        src_ref=source,
        dst_ref=target,
        send_sem=send,
        recv_sem=recv,
        device_id=place,
        device_id_type=MESH_ID,
    )


def spot(n_tile, n_obs, k):
    n = n_tile * n_obs
    me = lax.axis_index("tile") * n_obs + lax.axis_index("obs")
    peer = lax.rem(me + k, n)
    return me, peer, (peer // n_obs, lax.rem(peer, n_obs))


def greet_all(n_tile, n_obs):
    barrier = pltpu.get_barrier_semaphore()

    def greet(k, _):
        place = spot(n_tile, n_obs, k)[2]
        pl.semaphore_signal(barrier, inc=1, device_id=place, device_id_type=MESH_ID)
        return 0

    lax.fori_loop(1, n_tile * n_obs, greet, 0)


def await_all(n_tile, n_obs):
    pl.semaphore_wait(pltpu.get_barrier_semaphore(), n_tile * n_obs - 1)


def swap_start(n_tile, n_obs, x_ref, out_ref, sems):
    send_sem, recv_sem, own_sem = sems
    me = spot(n_tile, n_obs, 0)[0]

    def begin(k, _):
        _, peer, place = spot(n_tile, n_obs, k)
        remote(x_ref.at[peer], out_ref.at[me], send_sem.at[k], recv_sem.at[k], place).start()
        return 0

    lax.fori_loop(1, n_tile * n_obs, begin, 0)
    pltpu.make_async_copy(x_ref.at[me], out_ref.at[me], own_sem).start()


def swap_wait(n_tile, n_obs, x_ref, out_ref, sems):
    send_sem, recv_sem, own_sem = sems
    me = spot(n_tile, n_obs, 0)[0]

    def finish(k, _):
        _, peer, place = spot(n_tile, n_obs, k)
        remote(x_ref.at[peer], out_ref.at[me], send_sem.at[k], recv_sem.at[k], place).wait()
        return 0

    lax.fori_loop(1, n_tile * n_obs, finish, 0)
    pltpu.make_async_copy(x_ref.at[me], out_ref.at[me], own_sem).wait()


def swap_sems(n):
    return [pltpu.SemaphoreType.DMA((n,)), pltpu.SemaphoreType.DMA((n,)), pltpu.SemaphoreType.DMA]


def halo_copies(n_tile, n_obs, field, coefs, sems):
    tile, obs = lax.axis_index("tile"), lax.axis_index("obs")
    up, down = lax.rem(tile + n_tile - 1, n_tile), lax.rem(tile + 1, n_tile)
    west, east = lax.rem(obs + n_obs - 1, n_obs), lax.rem(obs + 1, n_obs)
    rows_ref, strips_ref, rows_out, strips_out, corners_out = field
    length = strips_ref.shape[1]
    top, end = pl.ds(0, 16), pl.ds(length - 16, 16)
    plan = [
        (rows_ref.at[pl.ds(0, 2)], rows_out.at[pl.ds(0, 2)], (up, obs)),
        (rows_ref.at[pl.ds(2, 2)], rows_out.at[pl.ds(2, 2)], (down, obs)),
        (strips_ref.at[pl.ds(0, 2)], strips_out.at[pl.ds(0, 2)], (tile, west)),
        (strips_ref.at[pl.ds(2, 2)], strips_out.at[pl.ds(2, 2)], (tile, east)),
        (strips_ref.at[0, top], corners_out.at[0], (up, west)),
        (strips_ref.at[0, end], corners_out.at[1], (down, west)),
        (strips_ref.at[2, top], corners_out.at[2], (up, east)),
        (strips_ref.at[2, end], corners_out.at[3], (down, east)),
    ]
    if coefs is not None:
        spread_ref, turned_ref, tiles_out = coefs
        plan += [
            (spread_ref.at[pl.ds(0, 8)], tiles_out.at[0], (up, obs)),
            (spread_ref.at[pl.ds(spread_ref.shape[0] - 8, 8)], tiles_out.at[1], (down, obs)),
            (turned_ref.at[0], tiles_out.at[2], (tile, west)),
            (turned_ref.at[1], tiles_out.at[3], (tile, east)),
            (turned_ref.at[0], tiles_out.at[4], (up, west)),
            (turned_ref.at[0], tiles_out.at[5], (down, west)),
            (turned_ref.at[1], tiles_out.at[6], (up, east)),
            (turned_ref.at[1], tiles_out.at[7], (down, east)),
        ]
    send_sem, recv_sem = sems
    return [
        remote(source, target, send_sem.at[i], recv_sem.at[i], peer)
        for i, (source, target, peer) in enumerate(plan)
    ]


def start_kernel(
    n_tile, n_obs, cap, control_ref, spread_ref, holder_ref, anchor_ref, frac_ref,
    pos_ref, req_ref, rows_out, strips_out, corners_out, own_out, tiles_out,
    ask, asked, rows_acc, strips_acc, rows_b, strips_b, turned, rows_in, strips_in, corners_in,
    tiles_in, *sems,
):
    step = pl.program_id(0)
    last = pl.num_programs(0) - 1
    _, rows_x, rows_y = control_ref.shape
    swap_set, halo_set = sems[:3], sems[3:]

    @pl.when(step == 0)
    def _():
        greet_all(n_tile, n_obs)
        request_kernel(cap, rows_y - 1, holder_ref, anchor_ref, frac_ref, ask, pos_ref)
        spread = spread_ref[...]
        square = jnp.concatenate([spread, jnp.zeros((rows_y - rows_x, rows_y), F32)], axis=0).T
        turned[0] = square[:8]
        turned[1] = square[rows_y - 8 :]
        strips_acc[...] = jnp.zeros_like(strips_acc)

    @pl.when(step == 1)
    def _():
        await_all(n_tile, n_obs)
        swap_start(n_tile, n_obs, ask, asked, swap_set)

    lane = lax.broadcasted_iota(jnp.int32, (rows_x, LANES), 1)
    first = pl.multiple_of(step * CHUNK, CHUNK)
    for k, x in enumerate((0, 1, rows_x - 2, rows_x - 1)):
        rows_acc[k, pl.ds(first, CHUNK), :] = control_ref[:, x, :]
    held = [strips_acc[k] for k in range(4)]
    for i in range(CHUNK):
        level = step * CHUNK + i
        moved = pltpu.roll(control_ref[i], level, 1)
        for k, shift in enumerate((0, 1, rows_y - 1, rows_y - 2)):
            held[k] = jnp.where(lane == lax.rem(level + shift, LANES), moved, held[k])
    for k in range(4):
        strips_acc[k] = held[k]

    @pl.when(step == last)
    def _():
        rows_b[...] = rows_acc[...].astype(BF16)
        for k, shift in enumerate((0, LANES - 1, 1, 2)):
            strip = strips_acc[k] if shift == 0 else pltpu.roll(strips_acc[k], shift, 1)
            strips_b[k] = strip.astype(BF16)
            if k % 2 == 0:
                own_out[k // 2] = strip
        copies = halo_copies(
            n_tile, n_obs, (rows_b, strips_b, rows_in, strips_in, corners_in),
            (spread_ref, turned, tiles_in), halo_set,
        )
        for copy in copies:
            copy.start()
        swap_wait(n_tile, n_obs, ask, asked, swap_set)
        req_ref[...] = jnp.concatenate(
            [asked[p][:, :cap] for p in range(n_tile * n_obs)], axis=1
        )
        for copy in copies:
            copy.wait()
        rows_out[...] = rows_in[...].astype(F32)
        strips_out[...] = strips_in[...].astype(F32)
        corners_out[...] = corners_in[...].astype(F32)
        tiles_out[...] = tiles_in[...]


def weight_fields(req, rows_x, rows_y):
    slots = req.shape[1]
    ax, ay = req[0:1].astype(jnp.int32), req[1:2].astype(jnp.int32)
    fx = req[2:3] + req[3:4] + req[4:5]
    fy = req[5:6] + req[6:7] + req[7:8]

    def ramp(size, place, frac):
        index = lax.broadcasted_iota(jnp.int32, (size, slots), 0)
        return jnp.where(index == place, 1.0 - frac, jnp.where(index == place + 1, frac, 0.0))

    return ramp(rows_x, ax, fx), ramp(rows_y, ay, fy)


def around(value, axis):
    size = value.shape[axis]
    return pltpu.roll(value, 1, axis) + pltpu.roll(value, size - 1, axis)


def strip_setup(adjoint, own_ref, strips_ref, corners_ref, tiles_ref, spread_ref, edge_ref):
    length, levels = own_ref.shape[1], own_ref.shape[2]
    index = lax.broadcasted_iota(jnp.int32, (8, levels), 0)

    def extended(base, low, high):
        return jnp.concatenate([base, jnp.where(index < 4, low, high)], axis=0)

    def plain(base):
        return jnp.concatenate([base, jnp.zeros((8, levels), F32)], axis=0)

    square = jnp.concatenate(
        [tiles_ref[t] for t in range(2, 8)] + [jnp.zeros((LANES - 48, LANES), F32)], axis=0
    ).T

    def coef(tile, row, first=0, size=length):
        at = 8 * (tile - 2) + row
        return jnp.broadcast_to(square[first : first + size, at : at + 1], (size, levels))

    size = spread_ref.shape[1]
    for side, (near, far, low, high, tile, rows, here) in enumerate(
        ((2, 3, 2, 3, 3, (7, 6), 0), (0, 1, 0, 1, 2, (0, 1), size - 1))
    ):
        s_near = extended(strips_ref[near], corners_ref[low, :8], corners_ref[high, 8:])
        s_far, s_own = plain(strips_ref[far]), plain(own_ref[side])
        d_near = extended(
            coef(tile, rows[0]),
            coef(4 + low, rows[0], 0, 8),
            coef(4 + high, rows[0], length - 8, 8),
        )
        if adjoint:
            d_far = plain(coef(tile, rows[1]))
            d_own = plain(jnp.broadcast_to(spread_ref[:, here : here + 1], (length, levels)))
            h_near = d_near * s_near
            first = s_near + around(h_near, 0) + d_far * s_far + d_own * s_own - 4.0 * h_near
            edge_ref[side] = h_near
            edge_ref[2 + side] = d_near * first
        else:
            first = s_near + d_near * (around(s_near, 0) + s_far + s_own - 4.0 * s_near)
            edge_ref[side] = s_near
            edge_ref[2 + side] = first


def extend_spread(spread_ref, tiles_ref):
    index = lax.broadcasted_iota(jnp.int32, (8, spread_ref.shape[1]), 0)
    return jnp.concatenate(
        [spread_ref[...], jnp.where(index < 4, tiles_ref[0], tiles_ref[1])], axis=0
    )


def extend_rows(block, rows_ref, level):
    index = lax.broadcasted_iota(jnp.int32, (8, block.shape[1]), 0)
    tile = jnp.zeros((8, block.shape[1]), F32)
    for k, place in enumerate((0, 1, 6, 7)):
        row = rows_ref[k, pl.ds(level, 1), :]
        tile = jnp.where(index == place, jnp.broadcast_to(row, tile.shape), tile)
    return jnp.concatenate([block, tile], axis=0)


def laplace(value, edge_ref, sweep, level):
    size = value.shape[1]
    lane = lax.broadcasted_iota(jnp.int32, value.shape, 1)
    west = pltpu.roll(edge_ref[2 * sweep], lax.rem(size - level, size), 1)
    east = pltpu.roll(edge_ref[2 * sweep + 1], size - 1 - level, 1)
    left = jnp.where(lane == 0, west, pltpu.roll(value, 1, 1))
    right = jnp.where(lane == size - 1, east, pltpu.roll(value, size - 1, 1))
    return around(value, 0) + left + right - 4.0 * value


def sweeps(adjoint, value, spread, edge_ref, level):
    for sweep in range(SWEEPS):
        if adjoint:
            value = value + laplace(spread * value, edge_ref, sweep, level)
        else:
            value = value + spread * laplace(value, edge_ref, sweep, level)
    return value


CHUNK = 8


def gather_level(block, y_ref, x_ref, out_ref, first):
    rows_x = x_ref.shape[0]
    got = jnp.dot(
        jnp.concatenate([block, block], axis=1), y_ref[...], preferred_element_type=F32
    )
    xs = x_ref[...]
    parts = [
        jnp.sum(got[i * rows_x : (i + 1) * rows_x] * xs, axis=0, keepdims=True)
        for i in range(CHUNK)
    ]
    out_ref[pl.ds(first, CHUNK), :] = jnp.concatenate(parts, axis=0)


def gather_kernel(
    n_tile, n_obs, cap, control_ref, bg_ref, rows_ref, own_ref, strips_ref, corners_ref, tiles_ref,
    spread_ref, req_ref, got_ref, x_ref, y_ref, d_ref, edge_ref, base_t, delta_t, inc_ref, sent, got,
    *sems,
):
    step = pl.program_id(0)
    rows_x, rows_y = spread_ref.shape

    @pl.when(step == 0)
    def _():
        greet_all(n_tile, n_obs)
        xs, ys = weight_fields(req_ref[...], rows_x, rows_y)
        x_ref[...] = xs
        high, low = split_two(ys)
        y_ref[pl.ds(0, rows_y), :] = high
        y_ref[pl.ds(rows_y, rows_y), :] = low
        d_ref[...] = extend_spread(spread_ref, tiles_ref)
        strip_setup(False, own_ref, strips_ref, corners_ref, tiles_ref, spread_ref, edge_ref)

    spread = d_ref[...]
    for i in range(CHUNK):
        level = step * CHUNK + i
        value = extend_rows(control_ref[i], rows_ref, level)
        value = sweeps(False, value, spread, edge_ref, level)
        inc_ref[pl.ds(i * rows_x, rows_x), :] = value[:rows_x].astype(BF16)
    first = pl.multiple_of(step * CHUNK, CHUNK)
    gather_level(bg_ref[...].reshape(CHUNK * rows_x, rows_y), y_ref, x_ref, base_t, first)
    gather_level(inc_ref[...], y_ref, x_ref, delta_t, first)

    @pl.when(step == pl.num_programs(0) - 1)
    def _():
        base, delta = base_t[...].T, delta_t[...].T
        for p in range(n_tile * n_obs):
            here = slice(p * cap, (p + 1) * cap)
            sent[p] = jnp.concatenate([base[here], delta[here]], axis=0).astype(BF16)
        await_all(n_tile, n_obs)
        swap_start(n_tile, n_obs, sent, got, sems)
        swap_wait(n_tile, n_obs, sent, got, sems)
        got_ref[...] = got[...]


def radiance_kernel(
    n_tile, n_obs, cap, rows_x, rows_y, pos_ref, got_ref, innov_ref, var_ref, w1_ref, b1_ref, w2_ref,
    b2_ref, w3_ref, req_ref, dep_ref, grad_t_ref, rows_out, strips_out, corners_out, own_out,
    sent, back, rows_b, strips_b, rows_in, strips_in, corners_in, *sems,
):
    greet_all(n_tile, n_obs)
    owners = n_tile * n_obs
    count = pos_ref.shape[0]
    both = got_ref.shape[0]
    pos = pos_ref[...]
    peer = jnp.floor((pos.astype(F32) + 0.5) / cap).astype(jnp.int32)
    place = pos + peer * cap
    lane = lax.broadcasted_iota(jnp.int32, (count, both), 1)
    got = got_ref[...]
    pick_b = (lane == place).astype(F32).astype(BF16)
    pick_d = (lane == place + cap).astype(F32).astype(BF16)
    base = jnp.dot(pick_b, got, preferred_element_type=F32).astype(BF16)
    delta = jnp.dot(pick_d, got, preferred_element_type=F32).astype(BF16)

    def forward(a, b):
        return jnp.dot(a, b, preferred_element_type=F32)

    def backward(a, b):
        return lax.dot_general(a, b, (((1,), (1,)), ((), ())), preferred_element_type=F32)

    w1, w2, w3t = w1_ref[...], w2_ref[...], w3_ref[...]
    h_one = jnp.tanh(forward(base, w1) + b1_ref[...])
    d_one = 1.0 - h_one * h_one
    h_two = jnp.tanh(forward(h_one.astype(BF16), w2) + b2_ref[...])
    d_two = 1.0 - h_two * h_two
    t_one = (d_one * forward(delta, w1)).astype(BF16)
    t_two = (d_two * forward(t_one, w2)).astype(BF16)
    dep = (backward(t_two, w3t) - innov_ref[...].T) * var_ref[...]
    dep_ref[...] = dep.T
    s_two = (d_two * forward(dep.astype(BF16), w3t)).astype(BF16)
    s_one = (d_one * backward(s_two, w2)).astype(BF16)
    grad = backward(s_one, w1).astype(BF16)
    slots = owners * cap
    spots = lax.broadcasted_iota(jnp.int32, (count, slots), 1)
    pick = (spots == pos).astype(F32).astype(BF16)
    packed = lax.dot_general(pick, grad, (((0,), (0,)), ((), ())), preferred_element_type=F32)
    for p in range(owners):
        sent[p] = packed[p * cap : (p + 1) * cap].astype(BF16)
    await_all(n_tile, n_obs)
    swap_start(n_tile, n_obs, sent, back, sems[:3])
    xs, ys = weight_fields(req_ref[...], rows_x, rows_y)
    swap_wait(n_tile, n_obs, sent, back, sems[:3])

    grad_f = jnp.concatenate([back[p].astype(F32) for p in range(owners)], axis=0)
    grad = grad_f.astype(BF16)
    grad_t = grad_f.T
    grad_t_ref[...] = grad_t
    grad_tb = grad_t.astype(BF16)
    for k, y in enumerate((0, 1, rows_y - 1, rows_y - 2)):
        high, low = split_two(xs * ys[y : y + 1])
        strip = forward(high, grad) + forward(low, grad)
        strips_b[k] = strip.astype(BF16)
        if k % 2 == 0:
            own_out[k // 2] = strip
    for k, x in enumerate((0, 1, rows_x - 2, rows_x - 1)):
        high, low = split_two(ys * xs[x : x + 1])
        rows_b[k] = (backward(grad_tb, high) + backward(grad_tb, low)).astype(BF16)
    copies = halo_copies(
        n_tile, n_obs, (rows_b, strips_b, rows_in, strips_in, corners_in), None, sems[3:]
    )
    for copy in copies:
        copy.start()
    for copy in copies:
        copy.wait()
    rows_out[...] = rows_in[...].astype(F32)
    strips_out[...] = strips_in[...].astype(F32)
    corners_out[...] = corners_in[...].astype(F32)


def adjoint_kernel(
    control_ref, grad_t_ref, req_ref, rows_ref, own_ref, strips_ref, corners_ref,
    tiles_ref, spread_ref,
    out_ref, x_ref, y_ref, d_ref, edge_ref, lhs_ref,
):
    step = pl.program_id(0)
    rows_x, rows_y = spread_ref.shape

    @pl.when(step == 0)
    def _():
        xs, ys = weight_fields(req_ref[...], rows_x, rows_y)
        x_ref[...] = xs
        high, low = split_two(ys.T)
        y_ref[:, pl.ds(0, rows_y)] = high
        y_ref[:, pl.ds(rows_y, rows_y)] = low
        d_ref[...] = extend_spread(spread_ref, tiles_ref)
        strip_setup(True, own_ref, strips_ref, corners_ref, tiles_ref, spread_ref, edge_ref)

    xs = x_ref[...]
    for i in range(CHUNK):
        row = grad_t_ref[pl.ds(i, 1), :]
        lhs_ref[pl.ds(i * rows_x, rows_x), :] = (xs * row).astype(BF16)
    both = jnp.dot(lhs_ref[...], y_ref[...], preferred_element_type=F32)
    field = both[:, :rows_y] + both[:, rows_y:]
    spread = d_ref[...]
    for i in range(CHUNK):
        level = step * CHUNK + i
        value = extend_rows(field[i * rows_x : (i + 1) * rows_x], rows_ref, level)
        value = sweeps(True, value, spread, edge_ref, level)
        out_ref[i] = control_ref[i] + value[:rows_x]


def whole(array):
    rank = len(array.shape)
    return pl.BlockSpec(array.shape, lambda i: (0,) * rank, pipeline_mode=pl.Buffered(1))


def per_device(
    n_tile, n_obs, control, background, spread, obs_holder, obs_anchor, obs_frac, innovation,
    inverse_var, w_first, b_first, w_second, b_second, w_third,
):
    levels, rows_x, rows_y = control.shape
    owners = n_tile * n_obs
    count = obs_anchor.shape[0]
    channels = innovation.shape[1]
    cap = 3 * count // owners
    slots = owners * cap

    steps = levels // CHUNK
    block = pl.BlockSpec((CHUNK, rows_x, rows_y), lambda i: (i, 0, 0))
    shape = jax.ShapeDtypeStruct
    pair, strip = shape((2, rows_x, levels), F32), shape((4, rows_x, levels), F32)
    row, corner = shape((4, levels, rows_y), F32), shape((4, 16, levels), F32)
    tiles = shape((8, 8, LANES), F32)
    landing = [
        pltpu.VMEM(row.shape, BF16),
        pltpu.VMEM(strip.shape, BF16),
        pltpu.VMEM(row.shape, BF16),
        pltpu.VMEM(strip.shape, BF16),
        pltpu.VMEM(corner.shape, BF16),
    ]
    several = pltpu.SemaphoreType.DMA

    outs = (shape((count, 1), jnp.int32), shape((8, slots), F32), row, strip, corner, pair, tiles)
    held = [spread, obs_holder, obs_anchor.reshape(1, count), obs_frac]
    pos, req, rows_c, strips_c, corners_c, own_c, tiles_c = pl.pallas_call(
        functools.partial(start_kernel, n_tile, n_obs, cap),
        grid=(steps,),
        out_shape=outs,
        in_specs=[block] + [whole(a) for a in held],
        out_specs=tuple(whole(a) for a in outs),
        scratch_shapes=[
            pltpu.VMEM((owners, 8, LANES), F32),
            pltpu.VMEM((owners, 8, LANES), F32),
            pltpu.VMEM(row.shape, F32),
            pltpu.VMEM(strip.shape, F32),
            *landing[:2],
            pltpu.VMEM((2, 8, LANES), F32),
            *landing[2:],
            pltpu.VMEM(tiles.shape, F32),
            *swap_sems(owners),
            several((16,)),
            several((16,)),
        ],
        compiler_params=pltpu.CompilerParams(collective_id=0, has_side_effects=True),
        name="start",
    )(control, *held)

    held = [rows_c, own_c, strips_c, corners_c, tiles_c, spread, req]
    column = shape((owners, 2 * cap, levels), BF16)
    got = pl.pallas_call(
        functools.partial(gather_kernel, n_tile, n_obs, cap),
        grid=(steps,),
        out_shape=column,
        in_specs=[block, block] + [whole(a) for a in held],
        out_specs=whole(column),
        scratch_shapes=[
            pltpu.VMEM((rows_x, slots), F32),
            pltpu.VMEM((2 * rows_y, slots), BF16),
            pltpu.VMEM((rows_x + 8, rows_y), F32),
            pltpu.VMEM((4, rows_x + 8, levels), F32),
            pltpu.VMEM((levels, slots), F32),
            pltpu.VMEM((levels, slots), F32),
            pltpu.VMEM((CHUNK * rows_x, rows_y), BF16),
            pltpu.VMEM(column.shape, BF16),
            pltpu.VMEM(column.shape, BF16),
            *swap_sems(owners),
        ],
        compiler_params=pltpu.CompilerParams(collective_id=1, has_side_effects=True),
        name="gather",
    )(control, background, *held)

    dep_t, grad_t, rows_a, strips_a, corners_a, own_a = pl.pallas_call(
        functools.partial(radiance_kernel, n_tile, n_obs, cap, rows_x, rows_y),
        out_shape=(
            shape((channels, count), F32), shape((levels, slots), F32), row, strip, corner, pair,
        ),
        in_specs=vmem(10),
        out_specs=tuple(vmem(6)),
        scratch_shapes=[
            pltpu.VMEM((owners, cap, levels), BF16),
            pltpu.VMEM((owners, cap, levels), BF16),
            *landing,
            *swap_sems(owners),
            several((8,)),
            several((8,)),
        ],
        compiler_params=pltpu.CompilerParams(collective_id=2, has_side_effects=True),
        name="radiances",
    )(
        pos, got.reshape(2 * slots, levels), innovation.T, inverse_var.reshape(1, -1), w_first,
        b_first.reshape(1, -1), w_second, b_second.reshape(1, -1), w_third.T, req,
    )

    held = [req, rows_a, own_a, strips_a, corners_a, tiles_c, spread]
    gradient = pl.pallas_call(
        adjoint_kernel,
        grid=(steps,),
        out_shape=jax.ShapeDtypeStruct(control.shape, F32),
        in_specs=[block, pl.BlockSpec((CHUNK, slots), lambda i: (i, 0))] + [whole(a) for a in held],
        out_specs=block,
        scratch_shapes=[
            pltpu.VMEM((rows_x, slots), F32),
            pltpu.VMEM((slots, 2 * rows_y), BF16),
            pltpu.VMEM((rows_x + 8, rows_y), F32),
            pltpu.VMEM((4, rows_x + 8, levels), F32),
            pltpu.VMEM((CHUNK * rows_x, slots), BF16),
        ],
        name="adjoint",
    )(control, grad_t, *held)
    return (dep_t.T, gradient)


def solution(mesh):
    n_tile, n_obs = mesh.shape["tile"], mesh.shape["obs"]
    return jax.shard_map(
        functools.partial(per_device, n_tile, n_obs),
        mesh=mesh,
        in_specs=(
            P(None, "tile", "obs"),
            P(None, "tile", "obs"),
            P("tile", "obs"),
            P(("tile", "obs"), None),
            P(("tile", "obs")),
            P(None, ("tile", "obs")),
            P(("tile", "obs"), None),
            P(),
            P(),
            P(),
            P(),
            P(),
            P(),
        ),
        out_specs=(P(("tile", "obs"), None), P(None, "tile", "obs")),
        check_vma=False,
    )
```

```python
import functools

import jax
import jax.numpy as jnp
from jax import lax
from jax.experimental import pallas as pl
from jax.experimental.pallas import tpu as pltpu
from jax.sharding import PartitionSpec as P

SWEEPS = 2
LANES = 128
MESH_ID = pl.DeviceIdType.MESH
F32 = jnp.float32
BF16 = jnp.bfloat16


def vmem(count):
    return [pl.BlockSpec(memory_space=pltpu.VMEM)] * count


def split_two(value):
    high = value.astype(BF16)
    return high, (value - high.astype(F32)).astype(BF16)


def request_kernel(cap, per_row, holder_ref, anchor_ref, frac_ref, req_ref, pos_ref):
    owners = req_ref.shape[0]
    count = holder_ref.shape[0]
    holder = holder_ref[...]
    marks = holder == lax.broadcasted_iota(jnp.int32, (count, owners), 1)
    marks = marks.astype(F32)
    tri = lax.broadcasted_iota(jnp.int32, (count, count), 0) > lax.broadcasted_iota(
        jnp.int32, (count, count), 1
    )
    before = jnp.dot(
        tri.astype(F32).astype(BF16), marks.astype(BF16), preferred_element_type=F32
    )
    rank = jnp.sum(before * marks, axis=1, keepdims=True).astype(jnp.int32)
    pos_ref[...] = holder * cap + rank
    slot = holder * LANES + rank
    anchor = anchor_ref[...].astype(F32)
    ax = jnp.floor((anchor + 0.5) / per_row)
    ay = anchor - ax * per_row
    rows = [ax, ay]
    for axis in range(2):
        value = frac_ref[pl.ds(axis, 1), :]
        for _ in range(3):
            part = value.astype(BF16).astype(F32)
            rows.append(part)
            value = value - part
    index = lax.broadcasted_iota(jnp.int32, (8, count), 0)
    fields = jnp.zeros((8, count), F32)
    for k, row in enumerate(rows):
        fields = jnp.where(index == k, jnp.broadcast_to(row, (8, count)), fields)
    fields = fields.astype(BF16)
    step = 8
    for first in range(0, owners, step):
        lane = lax.broadcasted_iota(jnp.int32, (count, step * LANES), 1) + first * LANES
        chosen = (slot == lane).astype(F32).astype(BF16)
        got = jnp.dot(fields, chosen, preferred_element_type=F32)
        for k in range(step):
            req_ref[first + k] = got[:, k * LANES : (k + 1) * LANES]


def remote(source, target, send, recv, place):
    return pltpu.make_async_remote_copy(
        src_ref=source,
        dst_ref=target,
        send_sem=send,
        recv_sem=recv,
        device_id=place,
        device_id_type=MESH_ID,
    )


def spot(n_tile, n_obs, k):
    n = n_tile * n_obs
    me = lax.axis_index("tile") * n_obs + lax.axis_index("obs")
    peer = lax.rem(me + k, n)
    return me, peer, (peer // n_obs, lax.rem(peer, n_obs))


def greet_all(n_tile, n_obs):
    barrier = pltpu.get_barrier_semaphore()

    def greet(k, _):
        place = spot(n_tile, n_obs, k)[2]
        pl.semaphore_signal(barrier, inc=1, device_id=place, device_id_type=MESH_ID)
        return 0

    lax.fori_loop(1, n_tile * n_obs, greet, 0)


def await_all(n_tile, n_obs):
    pl.semaphore_wait(pltpu.get_barrier_semaphore(), n_tile * n_obs - 1)


def swap_start(n_tile, n_obs, x_ref, out_ref, sems):
    send_sem, recv_sem, own_sem = sems
    me = spot(n_tile, n_obs, 0)[0]

    def begin(k, _):
        _, peer, place = spot(n_tile, n_obs, k)
        remote(x_ref.at[peer], out_ref.at[me], send_sem.at[k], recv_sem.at[k], place).start()
        return 0

    lax.fori_loop(1, n_tile * n_obs, begin, 0)
    pltpu.make_async_copy(x_ref.at[me], out_ref.at[me], own_sem).start()


def swap_wait(n_tile, n_obs, x_ref, out_ref, sems):
    send_sem, recv_sem, own_sem = sems
    me = spot(n_tile, n_obs, 0)[0]

    def finish(k, _):
        _, peer, place = spot(n_tile, n_obs, k)
        remote(x_ref.at[peer], out_ref.at[me], send_sem.at[k], recv_sem.at[k], place).wait()
        return 0

    lax.fori_loop(1, n_tile * n_obs, finish, 0)
    pltpu.make_async_copy(x_ref.at[me], out_ref.at[me], own_sem).wait()


def swap_sems(n):
    return [pltpu.SemaphoreType.DMA((n,)), pltpu.SemaphoreType.DMA((n,)), pltpu.SemaphoreType.DMA]


def halo_copies(n_tile, n_obs, field, coefs, sems):
    tile, obs = lax.axis_index("tile"), lax.axis_index("obs")
    up, down = lax.rem(tile + n_tile - 1, n_tile), lax.rem(tile + 1, n_tile)
    west, east = lax.rem(obs + n_obs - 1, n_obs), lax.rem(obs + 1, n_obs)
    rows_ref, strips_ref, rows_out, strips_out, corners_out = field
    length = strips_ref.shape[1]
    top, end = pl.ds(0, 16), pl.ds(length - 16, 16)
    plan = [
        (rows_ref.at[pl.ds(0, 2)], rows_out.at[pl.ds(0, 2)], (up, obs)),
        (rows_ref.at[pl.ds(2, 2)], rows_out.at[pl.ds(2, 2)], (down, obs)),
        (strips_ref.at[pl.ds(0, 2)], strips_out.at[pl.ds(0, 2)], (tile, west)),
        (strips_ref.at[pl.ds(2, 2)], strips_out.at[pl.ds(2, 2)], (tile, east)),
        (strips_ref.at[0, top], corners_out.at[0], (up, west)),
        (strips_ref.at[0, end], corners_out.at[1], (down, west)),
        (strips_ref.at[2, top], corners_out.at[2], (up, east)),
        (strips_ref.at[2, end], corners_out.at[3], (down, east)),
    ]
    if coefs is not None:
        spread_ref, turned_ref, tiles_out = coefs
        plan += [
            (spread_ref.at[pl.ds(0, 8)], tiles_out.at[0], (up, obs)),
            (spread_ref.at[pl.ds(spread_ref.shape[0] - 8, 8)], tiles_out.at[1], (down, obs)),
            (turned_ref.at[0], tiles_out.at[2], (tile, west)),
            (turned_ref.at[1], tiles_out.at[3], (tile, east)),
            (turned_ref.at[0], tiles_out.at[4], (up, west)),
            (turned_ref.at[0], tiles_out.at[5], (down, west)),
            (turned_ref.at[1], tiles_out.at[6], (up, east)),
            (turned_ref.at[1], tiles_out.at[7], (down, east)),
        ]
    send_sem, recv_sem = sems
    return [
        remote(source, target, send_sem.at[i], recv_sem.at[i], peer)
        for i, (source, target, peer) in enumerate(plan)
    ]


def start_kernel(
    n_tile, n_obs, cap, control_ref, spread_ref, holder_ref, anchor_ref, frac_ref,
    pos_ref, req_ref, rows_out, strips_out, corners_out, own_out, tiles_out,
    ask, asked, rows_acc, strips_acc, rows_b, strips_b, turned, rows_in, strips_in, corners_in,
    tiles_in, *sems,
):
    step = pl.program_id(0)
    last = pl.num_programs(0) - 1
    _, rows_x, rows_y = control_ref.shape
    swap_set, halo_set = sems[:3], sems[3:]

    @pl.when(step == 0)
    def _():
        greet_all(n_tile, n_obs)
        request_kernel(cap, rows_y - 1, holder_ref, anchor_ref, frac_ref, ask, pos_ref)
        spread = spread_ref[...]
        square = jnp.concatenate([spread, jnp.zeros((rows_y - rows_x, rows_y), F32)], axis=0).T
        turned[0] = square[:8]
        turned[1] = square[rows_y - 8 :]
        strips_acc[...] = jnp.zeros_like(strips_acc)

    @pl.when(step == 1)
    def _():
        await_all(n_tile, n_obs)
        swap_start(n_tile, n_obs, ask, asked, swap_set)

    lane = lax.broadcasted_iota(jnp.int32, (rows_x, LANES), 1)
    first = pl.multiple_of(step * CHUNK, CHUNK)
    for k, x in enumerate((0, 1, rows_x - 2, rows_x - 1)):
        rows_acc[k, pl.ds(first, CHUNK), :] = control_ref[:, x, :]
    held = [strips_acc[k] for k in range(4)]
    for i in range(CHUNK):
        level = step * CHUNK + i
        moved = pltpu.roll(control_ref[i], level, 1)
        for k, shift in enumerate((0, 1, rows_y - 1, rows_y - 2)):
            held[k] = jnp.where(lane == lax.rem(level + shift, LANES), moved, held[k])
    for k in range(4):
        strips_acc[k] = held[k]

    @pl.when(step == last)
    def _():
        rows_b[...] = rows_acc[...].astype(BF16)
        for k, shift in enumerate((0, LANES - 1, 1, 2)):
            strip = strips_acc[k] if shift == 0 else pltpu.roll(strips_acc[k], shift, 1)
            strips_b[k] = strip.astype(BF16)
            if k % 2 == 0:
                own_out[k // 2] = strip
        copies = halo_copies(
            n_tile, n_obs, (rows_b, strips_b, rows_in, strips_in, corners_in),
            (spread_ref, turned, tiles_in), halo_set,
        )
        for copy in copies:
            copy.start()
        swap_wait(n_tile, n_obs, ask, asked, swap_set)
        req_ref[...] = jnp.concatenate(
            [asked[p][:, :cap] for p in range(n_tile * n_obs)], axis=1
        )
        for copy in copies:
            copy.wait()
        rows_out[...] = rows_in[...].astype(F32)
        strips_out[...] = strips_in[...].astype(F32)
        corners_out[...] = corners_in[...].astype(F32)
        tiles_out[...] = tiles_in[...]


def weight_fields(req, rows_x, rows_y):
    slots = req.shape[1]
    ax, ay = req[0:1].astype(jnp.int32), req[1:2].astype(jnp.int32)
    fx = req[2:3] + req[3:4] + req[4:5]
    fy = req[5:6] + req[6:7] + req[7:8]

    def ramp(size, place, frac):
        index = lax.broadcasted_iota(jnp.int32, (size, slots), 0)
        return jnp.where(index == place, 1.0 - frac, jnp.where(index == place + 1, frac, 0.0))

    return ramp(rows_x, ax, fx), ramp(rows_y, ay, fy)


def around(value, axis):
    size = value.shape[axis]
    return pltpu.roll(value, 1, axis) + pltpu.roll(value, size - 1, axis)


def strip_setup(adjoint, own_ref, strips_ref, corners_ref, tiles_ref, spread_ref):
    length, levels = own_ref.shape[1], own_ref.shape[2]
    index = lax.broadcasted_iota(jnp.int32, (8, levels), 0)

    def extended(base, low, high):
        return jnp.concatenate([base, jnp.where(index < 4, low, high)], axis=0)

    def plain(base):
        return jnp.concatenate([base, jnp.zeros((8, levels), F32)], axis=0)

    square = jnp.concatenate(
        [tiles_ref[t] for t in range(2, 8)] + [jnp.zeros((LANES - 48, LANES), F32)], axis=0
    ).T

    def coef(tile, row, first=0, size=length):
        at = 8 * (tile - 2) + row
        return jnp.broadcast_to(square[first : first + size, at : at + 1], (size, levels))

    def column(ref, at, size):
        return jnp.broadcast_to(ref[:, at : at + 1], (size, levels))

    size = spread_ref.shape[1]
    parts = []
    for side, (near, far, low, high, tile, rows, here, there) in enumerate(
        ((2, 3, 2, 3, 3, (7, 6), 0, 1), (0, 1, 0, 1, 2, (0, 1), size - 1, size - 2))
    ):
        s_near = extended(strips_ref[near], corners_ref[low, :8], corners_ref[high, 8:])
        s_far, s_own = plain(strips_ref[far]), plain(own_ref[side])
        d_near = extended(
            coef(tile, rows[0]),
            coef(4 + low, rows[0], 0, 8),
            coef(4 + high, rows[0], length - 8, 8),
        )
        d_here = extended(
            column(spread_ref, here, length),
            column(tiles_ref.at[0], here, 8),
            column(tiles_ref.at[1], here, 8),
        )
        if adjoint:
            d_far = plain(coef(tile, rows[1]))
            once = d_near * s_near
            first = s_near + around(once, 0) + d_far * s_far + d_here * s_own - 4.0 * once
            scaled = d_here * once
            parts += [once + around(scaled, 0) - 4.0 * scaled + d_near * first, scaled]
        else:
            first = s_near + d_near * (around(s_near, 0) + s_far + s_own - 4.0 * s_near)
            once = d_here * s_near
            parts += [
                once + d_here * (around(once, 0) - 4.0 * once + first),
                plain(column(spread_ref, there, length)) * once,
            ]
    return [part[:length] for part in parts]


PAD = 8


def fill_spread(spread_ref, tiles_ref, d_ref):
    rows_x = spread_ref.shape[0]
    d_ref[pl.ds(0, PAD), :] = tiles_ref[1]
    d_ref[pl.ds(PAD, rows_x), :] = spread_ref[...]
    d_ref[pl.ds(PAD + rows_x, PAD), :] = tiles_ref[0]


def rim_tiles(rows_ref, level, size):
    index = lax.broadcasted_iota(jnp.int32, (PAD, size), 0)

    def row(k):
        return jnp.broadcast_to(rows_ref[k, pl.ds(level, 1), :], (PAD, size))

    return jnp.where(index < 7, row(2), row(3)), jnp.where(index < 1, row(0), row(1))


def laplace(buf, i, first, count):
    centre = buf[i, pl.ds(first, count), :]
    size = centre.shape[1]
    lane = lax.broadcasted_iota(jnp.int32, centre.shape, 1)
    total = buf[i, pl.ds(first - 1, count), :] + buf[i, pl.ds(first + 1, count), :]
    total = total + jnp.where(lane == 0, 0.0, pltpu.roll(centre, 1, 1))
    total = total + jnp.where(lane == size - 1, 0.0, pltpu.roll(centre, size - 1, 1))
    return centre, total - 4.0 * centre


CHUNK = 8


def gather_level(block, y_ref, x_ref, out_ref, first):
    rows_x = x_ref.shape[0]
    got = jnp.dot(
        jnp.concatenate([block, block], axis=1), y_ref[...], preferred_element_type=F32
    )
    xs = x_ref[...]
    parts = [
        jnp.sum(got[i * rows_x : (i + 1) * rows_x] * xs, axis=0, keepdims=True)
        for i in range(CHUNK)
    ]
    out_ref[pl.ds(first, CHUNK), :] = jnp.concatenate(parts, axis=0)


def gather_kernel(
    n_tile, n_obs, cap, control_ref, bg_ref, rows_ref, own_ref, strips_ref, corners_ref, tiles_ref,
    spread_ref, req_ref, got_ref, x_ref, y_ref, d_ref, fix_ref, base_t, delta_t, inc_ref, buf, buf_b,
    sent, got, *sems,
):
    step = pl.program_id(0)
    rows_x, rows_y = spread_ref.shape

    @pl.when(step == 0)
    def _():
        greet_all(n_tile, n_obs)
        xs, ys = weight_fields(req_ref[...], rows_x, rows_y)
        x_ref[...] = xs
        high, low = split_two(ys)
        y_ref[pl.ds(0, rows_y), :] = high
        y_ref[pl.ds(rows_y, rows_y), :] = low
        fill_spread(spread_ref, tiles_ref, d_ref)
        parts = strip_setup(False, own_ref, strips_ref, corners_ref, tiles_ref, spread_ref)
        rims = (0, 1, rows_y - 1, rows_y - 2)
        weights = jnp.concatenate([xs * ys[y : y + 1] for y in rims], axis=0)
        fix_ref[...] = lax.dot_general(
            weights.astype(BF16),
            jnp.concatenate(parts, axis=0).astype(BF16),
            (((0,), (0,)), ((), ())),
            preferred_element_type=F32,
        )

    wide = rows_x + PAD
    for i in range(CHUNK):
        level = step * CHUNK + i
        north, south = rim_tiles(rows_ref, level, rows_y)
        buf[i, pl.ds(0, PAD), :] = north
        buf[i, pl.ds(PAD, rows_x), :] = control_ref[i]
        buf[i, pl.ds(PAD + rows_x, PAD), :] = south
        centre, total = laplace(buf, i, PAD - 1, wide)
        buf_b[i, pl.ds(PAD - 1, wide), :] = centre + d_ref[pl.ds(PAD - 1, wide), :] * total
        centre, total = laplace(buf_b, i, PAD, rows_x)
        value = centre + d_ref[pl.ds(PAD, rows_x), :] * total
        inc_ref[pl.ds(i * rows_x, rows_x), :] = value.astype(BF16)
    first = pl.multiple_of(step * CHUNK, CHUNK)
    gather_level(bg_ref[...].reshape(CHUNK * rows_x, rows_y), y_ref, x_ref, base_t, first)
    gather_level(inc_ref[...], y_ref, x_ref, delta_t, first)

    @pl.when(step == pl.num_programs(0) - 1)
    def _():
        base, delta = base_t[...].T, delta_t[...].T + fix_ref[...]
        for p in range(n_tile * n_obs):
            here = slice(p * cap, (p + 1) * cap)
            sent[p] = jnp.concatenate([base[here], delta[here]], axis=0).astype(BF16)
        await_all(n_tile, n_obs)
        swap_start(n_tile, n_obs, sent, got, sems)
        swap_wait(n_tile, n_obs, sent, got, sems)
        got_ref[...] = got[...]


def radiance_kernel(
    n_tile, n_obs, cap, rows_x, rows_y, pos_ref, got_ref, innov_ref, var_ref, w1_ref, b1_ref, w2_ref,
    b2_ref, w3_ref, req_ref, dep_ref, grad_t_ref, rows_out, strips_out, corners_out, own_out,
    sent, back, rows_b, strips_b, rows_in, strips_in, corners_in, *sems,
):
    greet_all(n_tile, n_obs)
    owners = n_tile * n_obs
    count = pos_ref.shape[0]
    both = got_ref.shape[0]
    pos = pos_ref[...]
    peer = jnp.floor((pos.astype(F32) + 0.5) / cap).astype(jnp.int32)
    place = pos + peer * cap
    lane = lax.broadcasted_iota(jnp.int32, (count, both), 1)
    got = got_ref[...]
    pick_b = (lane == place).astype(F32).astype(BF16)
    pick_d = (lane == place + cap).astype(F32).astype(BF16)
    base = jnp.dot(pick_b, got, preferred_element_type=F32).astype(BF16)
    delta = jnp.dot(pick_d, got, preferred_element_type=F32).astype(BF16)

    def forward(a, b):
        return jnp.dot(a, b, preferred_element_type=F32)

    def backward(a, b):
        return lax.dot_general(a, b, (((1,), (1,)), ((), ())), preferred_element_type=F32)

    w1, w2, w3t = w1_ref[...], w2_ref[...], w3_ref[...]
    h_one = jnp.tanh(forward(base, w1) + b1_ref[...])
    d_one = 1.0 - h_one * h_one
    h_two = jnp.tanh(forward(h_one.astype(BF16), w2) + b2_ref[...])
    d_two = 1.0 - h_two * h_two
    t_one = (d_one * forward(delta, w1)).astype(BF16)
    t_two = (d_two * forward(t_one, w2)).astype(BF16)
    dep = (backward(t_two, w3t) - innov_ref[...].T) * var_ref[...]
    dep_ref[...] = dep.T
    s_two = (d_two * forward(dep.astype(BF16), w3t)).astype(BF16)
    s_one = (d_one * backward(s_two, w2)).astype(BF16)
    grad = backward(s_one, w1).astype(BF16)
    slots = owners * cap
    spots = lax.broadcasted_iota(jnp.int32, (count, slots), 1)
    pick = (spots == pos).astype(F32).astype(BF16)
    packed = lax.dot_general(pick, grad, (((0,), (0,)), ((), ())), preferred_element_type=F32)
    for p in range(owners):
        sent[p] = packed[p * cap : (p + 1) * cap].astype(BF16)
    await_all(n_tile, n_obs)
    swap_start(n_tile, n_obs, sent, back, sems[:3])
    xs, ys = weight_fields(req_ref[...], rows_x, rows_y)
    swap_wait(n_tile, n_obs, sent, back, sems[:3])

    grad_f = jnp.concatenate([back[p].astype(F32) for p in range(owners)], axis=0)
    grad = grad_f.astype(BF16)
    grad_t = grad_f.T
    grad_t_ref[...] = grad_t
    grad_tb = grad_t.astype(BF16)
    for k, y in enumerate((0, 1, rows_y - 1, rows_y - 2)):
        high, low = split_two(xs * ys[y : y + 1])
        strip = forward(high, grad) + forward(low, grad)
        strips_b[k] = strip.astype(BF16)
        if k % 2 == 0:
            own_out[k // 2] = strip
    for k, x in enumerate((0, 1, rows_x - 2, rows_x - 1)):
        high, low = split_two(ys * xs[x : x + 1])
        rows_b[k] = (backward(grad_tb, high) + backward(grad_tb, low)).astype(BF16)
    copies = halo_copies(
        n_tile, n_obs, (rows_b, strips_b, rows_in, strips_in, corners_in), None, sems[3:]
    )
    for copy in copies:
        copy.start()
    for copy in copies:
        copy.wait()
    rows_out[...] = rows_in[...].astype(F32)
    strips_out[...] = strips_in[...].astype(F32)
    corners_out[...] = corners_in[...].astype(F32)


def adjoint_kernel(
    control_ref, grad_t_ref, req_ref, rows_ref, own_ref, strips_ref, corners_ref,
    tiles_ref, spread_ref,
    out_ref, x_ref, y_ref, d_ref, fix_ref, lhs_ref, buf, buf_b, buf_f,
):
    step = pl.program_id(0)
    rows_x, rows_y = spread_ref.shape

    @pl.when(step == 0)
    def _():
        xs, ys = weight_fields(req_ref[...], rows_x, rows_y)
        x_ref[...] = xs
        high, low = split_two(ys.T)
        y_ref[:, pl.ds(0, rows_y)] = high
        y_ref[:, pl.ds(rows_y, rows_y)] = low
        fill_spread(spread_ref, tiles_ref, d_ref)
        parts = strip_setup(True, own_ref, strips_ref, corners_ref, tiles_ref, spread_ref)
        shifts = (0, 1, rows_y - 1, rows_y - 2)
        moved = [p if t == 0 else pltpu.roll(p, t, 1) for p, t in zip(parts, shifts)]
        lane = lax.broadcasted_iota(jnp.int32, (rows_x, rows_y), 1)
        for r in range(4):
            key = lax.rem(lane + (4 - r), 4)
            mixed = jnp.where(key == 0, moved[0], jnp.where(key == 1, moved[1], moved[3]))
            fix_ref[r] = jnp.where(key == 3, moved[2], mixed)

    xs = x_ref[...]
    for i in range(CHUNK):
        row = grad_t_ref[pl.ds(i, 1), :]
        lhs_ref[pl.ds(i * rows_x, rows_x), :] = (xs * row).astype(BF16)
    both = jnp.dot(lhs_ref[...], y_ref[...], preferred_element_type=F32)
    field = both[:, :rows_y] + both[:, rows_y:]
    wide = rows_x + PAD
    lane = lax.broadcasted_iota(jnp.int32, (rows_x, rows_y), 1)
    rim = (lane < 2) | (lane >= rows_y - 2)
    d_top, d_own, d_end = (
        d_ref[pl.ds(0, PAD), :], d_ref[pl.ds(PAD, rows_x), :], d_ref[pl.ds(PAD + rows_x, PAD), :],
    )
    for i in range(CHUNK):
        level = step * CHUNK + i
        north, south = rim_tiles(rows_ref, level, rows_y)
        own = field[i * rows_x : (i + 1) * rows_x]
        buf_f[i, pl.ds(0, PAD), :] = north
        buf_f[i, pl.ds(PAD, rows_x), :] = own
        buf_f[i, pl.ds(PAD + rows_x, PAD), :] = south
        buf[i, pl.ds(0, PAD), :] = d_top * north
        buf[i, pl.ds(PAD, rows_x), :] = d_own * own
        buf[i, pl.ds(PAD + rows_x, PAD), :] = d_end * south
        total = laplace(buf, i, PAD - 1, wide)[1]
        once = buf_f[i, pl.ds(PAD - 1, wide), :] + total
        buf_f[i, pl.ds(PAD - 1, wide), :] = once
        buf_b[i, pl.ds(PAD - 1, wide), :] = d_ref[pl.ds(PAD - 1, wide), :] * once
        total = laplace(buf_b, i, PAD, rows_x)[1]
        fix = pltpu.roll(fix_ref[i % 4], lax.rem(rows_y - level, rows_y), 1)
        value = buf_f[i, pl.ds(PAD, rows_x), :] + total + jnp.where(rim, fix, 0.0)
        out_ref[i] = control_ref[i] + value


def whole(array):
    rank = len(array.shape)
    return pl.BlockSpec(array.shape, lambda i: (0,) * rank, pipeline_mode=pl.Buffered(1))


def per_device(
    n_tile, n_obs, control, background, spread, obs_holder, obs_anchor, obs_frac, innovation,
    inverse_var, w_first, b_first, w_second, b_second, w_third,
):
    levels, rows_x, rows_y = control.shape
    owners = n_tile * n_obs
    count = obs_anchor.shape[0]
    channels = innovation.shape[1]
    cap = 3 * count // owners
    slots = owners * cap

    steps = levels // CHUNK
    block = pl.BlockSpec((CHUNK, rows_x, rows_y), lambda i: (i, 0, 0))
    shape = jax.ShapeDtypeStruct
    pair, strip = shape((2, rows_x, levels), F32), shape((4, rows_x, levels), F32)
    row, corner = shape((4, levels, rows_y), F32), shape((4, 16, levels), F32)
    tiles = shape((8, 8, LANES), F32)
    landing = [
        pltpu.VMEM(row.shape, BF16),
        pltpu.VMEM(strip.shape, BF16),
        pltpu.VMEM(row.shape, BF16),
        pltpu.VMEM(strip.shape, BF16),
        pltpu.VMEM(corner.shape, BF16),
    ]
    several = pltpu.SemaphoreType.DMA
    padded = pltpu.VMEM((CHUNK, rows_x + 2 * PAD, rows_y), F32)

    outs = (shape((count, 1), jnp.int32), shape((8, slots), F32), row, strip, corner, pair, tiles)
    held = [spread, obs_holder, obs_anchor.reshape(1, count), obs_frac]
    pos, req, rows_c, strips_c, corners_c, own_c, tiles_c = pl.pallas_call(
        functools.partial(start_kernel, n_tile, n_obs, cap),
        grid=(steps,),
        out_shape=outs,
        in_specs=[block] + [whole(a) for a in held],
        out_specs=tuple(whole(a) for a in outs),
        scratch_shapes=[
            pltpu.VMEM((owners, 8, LANES), F32),
            pltpu.VMEM((owners, 8, LANES), F32),
            pltpu.VMEM(row.shape, F32),
            pltpu.VMEM(strip.shape, F32),
            *landing[:2],
            pltpu.VMEM((2, 8, LANES), F32),
            *landing[2:],
            pltpu.VMEM(tiles.shape, F32),
            *swap_sems(owners),
            several((16,)),
            several((16,)),
        ],
        compiler_params=pltpu.CompilerParams(collective_id=0, has_side_effects=True),
        name="start",
    )(control, *held)

    held = [rows_c, own_c, strips_c, corners_c, tiles_c, spread, req]
    column = shape((owners, 2 * cap, levels), BF16)
    got = pl.pallas_call(
        functools.partial(gather_kernel, n_tile, n_obs, cap),
        grid=(steps,),
        out_shape=column,
        in_specs=[block, block] + [whole(a) for a in held],
        out_specs=whole(column),
        scratch_shapes=[
            pltpu.VMEM((rows_x, slots), F32),
            pltpu.VMEM((2 * rows_y, slots), BF16),
            pltpu.VMEM((rows_x + 2 * PAD, rows_y), F32),
            pltpu.VMEM((slots, levels), F32),
            pltpu.VMEM((levels, slots), F32),
            pltpu.VMEM((levels, slots), F32),
            pltpu.VMEM((CHUNK * rows_x, rows_y), BF16),
            padded,
            padded,
            pltpu.VMEM(column.shape, BF16),
            pltpu.VMEM(column.shape, BF16),
            *swap_sems(owners),
        ],
        compiler_params=pltpu.CompilerParams(collective_id=1, has_side_effects=True),
        name="gather",
    )(control, background, *held)

    dep_t, grad_t, rows_a, strips_a, corners_a, own_a = pl.pallas_call(
        functools.partial(radiance_kernel, n_tile, n_obs, cap, rows_x, rows_y),
        out_shape=(
            shape((channels, count), F32), shape((levels, slots), F32), row, strip, corner, pair,
        ),
        in_specs=vmem(10),
        out_specs=tuple(vmem(6)),
        scratch_shapes=[
            pltpu.VMEM((owners, cap, levels), BF16),
            pltpu.VMEM((owners, cap, levels), BF16),
            *landing,
            *swap_sems(owners),
            several((8,)),
            several((8,)),
        ],
        compiler_params=pltpu.CompilerParams(collective_id=2, has_side_effects=True),
        name="radiances",
    )(
        pos, got.reshape(2 * slots, levels), innovation.T, inverse_var.reshape(1, -1), w_first,
        b_first.reshape(1, -1), w_second, b_second.reshape(1, -1), w_third.T, req,
    )

    held = [req, rows_a, own_a, strips_a, corners_a, tiles_c, spread]
    gradient = pl.pallas_call(
        adjoint_kernel,
        grid=(steps,),
        out_shape=jax.ShapeDtypeStruct(control.shape, F32),
        in_specs=[block, pl.BlockSpec((CHUNK, slots), lambda i: (i, 0))] + [whole(a) for a in held],
        out_specs=block,
        scratch_shapes=[
            pltpu.VMEM((rows_x, slots), F32),
            pltpu.VMEM((slots, 2 * rows_y), BF16),
            pltpu.VMEM((rows_x + 2 * PAD, rows_y), F32),
            pltpu.VMEM((4, rows_x, levels), F32),
            pltpu.VMEM((CHUNK * rows_x, slots), BF16),
            padded,
            padded,
            padded,
        ],
        name="adjoint",
    )(control, grad_t, *held)
    return (dep_t.T, gradient)


def solution(mesh):
    n_tile, n_obs = mesh.shape["tile"], mesh.shape["obs"]
    return jax.shard_map(
        functools.partial(per_device, n_tile, n_obs),
        mesh=mesh,
        in_specs=(
            P(None, "tile", "obs"),
            P(None, "tile", "obs"),
            P("tile", "obs"),
            P(("tile", "obs"), None),
            P(("tile", "obs")),
            P(None, ("tile", "obs")),
            P(("tile", "obs"), None),
            P(),
            P(),
            P(),
            P(),
            P(),
            P(),
        ),
        out_specs=(P(("tile", "obs"), None), P(None, "tile", "obs")),
        check_vma=False,
    )
```

```python
import functools

import jax
import jax.numpy as jnp
from jax import lax
from jax.experimental import pallas as pl
from jax.experimental.pallas import tpu as pltpu
from jax.sharding import PartitionSpec as P

SWEEPS = 2
LANES = 128
MESH_ID = pl.DeviceIdType.MESH
F32 = jnp.float32
BF16 = jnp.bfloat16


def vmem(count):
    return [pl.BlockSpec(memory_space=pltpu.VMEM)] * count


def split_two(value):
    high = value.astype(BF16)
    return high, (value - high.astype(F32)).astype(BF16)


def request_kernel(cap, per_row, holder_ref, anchor_ref, frac_ref, req_ref, pos_ref):
    owners = req_ref.shape[0]
    count = holder_ref.shape[0]
    holder = holder_ref[...]
    marks = holder == lax.broadcasted_iota(jnp.int32, (count, owners), 1)
    marks = marks.astype(F32)
    tri = lax.broadcasted_iota(jnp.int32, (count, count), 0) > lax.broadcasted_iota(
        jnp.int32, (count, count), 1
    )
    before = jnp.dot(
        tri.astype(F32).astype(BF16), marks.astype(BF16), preferred_element_type=F32
    )
    rank = jnp.sum(before * marks, axis=1, keepdims=True).astype(jnp.int32)
    pos_ref[...] = holder * cap + rank
    slot = holder * LANES + rank
    anchor = anchor_ref[...].astype(F32)
    ax = jnp.floor((anchor + 0.5) / per_row)
    ay = anchor - ax * per_row
    rows = [ax, ay]
    for axis in range(2):
        value = frac_ref[pl.ds(axis, 1), :]
        for _ in range(3):
            part = value.astype(BF16).astype(F32)
            rows.append(part)
            value = value - part
    index = lax.broadcasted_iota(jnp.int32, (8, count), 0)
    fields = jnp.zeros((8, count), F32)
    for k, row in enumerate(rows):
        fields = jnp.where(index == k, jnp.broadcast_to(row, (8, count)), fields)
    fields = fields.astype(BF16)
    step = 8
    for first in range(0, owners, step):
        lane = lax.broadcasted_iota(jnp.int32, (count, step * LANES), 1) + first * LANES
        chosen = (slot == lane).astype(F32).astype(BF16)
        got = jnp.dot(fields, chosen, preferred_element_type=F32)
        for k in range(step):
            req_ref[first + k] = got[:, k * LANES : (k + 1) * LANES]


def remote(source, target, send, recv, place):
    return pltpu.make_async_remote_copy(
        src_ref=source,
        dst_ref=target,
        send_sem=send,
        recv_sem=recv,
        device_id=place,
        device_id_type=MESH_ID,
    )


def spot(n_tile, n_obs, k):
    n = n_tile * n_obs
    me = lax.axis_index("tile") * n_obs + lax.axis_index("obs")
    peer = lax.rem(me + k, n)
    return me, peer, (peer // n_obs, lax.rem(peer, n_obs))


def greet_all(n_tile, n_obs):
    barrier = pltpu.get_barrier_semaphore()

    def greet(k, _):
        place = spot(n_tile, n_obs, k)[2]
        pl.semaphore_signal(barrier, inc=1, device_id=place, device_id_type=MESH_ID)
        return 0

    lax.fori_loop(1, n_tile * n_obs, greet, 0)


def await_all(n_tile, n_obs):
    pl.semaphore_wait(pltpu.get_barrier_semaphore(), n_tile * n_obs - 1)


def swap_start(n_tile, n_obs, x_ref, out_ref, sems):
    send_sem, recv_sem, own_sem = sems
    me = spot(n_tile, n_obs, 0)[0]

    def begin(k, _):
        _, peer, place = spot(n_tile, n_obs, k)
        remote(x_ref.at[peer], out_ref.at[me], send_sem.at[k], recv_sem.at[k], place).start()
        return 0

    lax.fori_loop(1, n_tile * n_obs, begin, 0)
    pltpu.make_async_copy(x_ref.at[me], out_ref.at[me], own_sem).start()


def swap_wait(n_tile, n_obs, x_ref, out_ref, sems):
    send_sem, recv_sem, own_sem = sems
    me = spot(n_tile, n_obs, 0)[0]

    def finish(k, _):
        _, peer, place = spot(n_tile, n_obs, k)
        remote(x_ref.at[peer], out_ref.at[me], send_sem.at[k], recv_sem.at[k], place).wait()
        return 0

    lax.fori_loop(1, n_tile * n_obs, finish, 0)
    pltpu.make_async_copy(x_ref.at[me], out_ref.at[me], own_sem).wait()


def swap_sems(n):
    return [pltpu.SemaphoreType.DMA((n,)), pltpu.SemaphoreType.DMA((n,)), pltpu.SemaphoreType.DMA]


def halo_copies(n_tile, n_obs, field, coefs, sems):
    tile, obs = lax.axis_index("tile"), lax.axis_index("obs")
    up, down = lax.rem(tile + n_tile - 1, n_tile), lax.rem(tile + 1, n_tile)
    west, east = lax.rem(obs + n_obs - 1, n_obs), lax.rem(obs + 1, n_obs)
    rows_ref, strips_ref, rows_out, strips_out, corners_out = field
    length = strips_ref.shape[1]
    top, end = pl.ds(0, 16), pl.ds(length - 16, 16)
    plan = [
        (rows_ref.at[pl.ds(0, 2)], rows_out.at[pl.ds(0, 2)], (up, obs)),
        (rows_ref.at[pl.ds(2, 2)], rows_out.at[pl.ds(2, 2)], (down, obs)),
        (strips_ref.at[pl.ds(0, 2)], strips_out.at[pl.ds(0, 2)], (tile, west)),
        (strips_ref.at[pl.ds(2, 2)], strips_out.at[pl.ds(2, 2)], (tile, east)),
        (strips_ref.at[0, top], corners_out.at[0], (up, west)),
        (strips_ref.at[0, end], corners_out.at[1], (down, west)),
        (strips_ref.at[2, top], corners_out.at[2], (up, east)),
        (strips_ref.at[2, end], corners_out.at[3], (down, east)),
    ]
    if coefs is not None:
        spread_ref, turned_ref, tiles_out = coefs
        plan += [
            (spread_ref.at[pl.ds(0, 8)], tiles_out.at[0], (up, obs)),
            (spread_ref.at[pl.ds(spread_ref.shape[0] - 8, 8)], tiles_out.at[1], (down, obs)),
            (turned_ref.at[0], tiles_out.at[2], (tile, west)),
            (turned_ref.at[1], tiles_out.at[3], (tile, east)),
            (turned_ref.at[0], tiles_out.at[4], (up, west)),
            (turned_ref.at[0], tiles_out.at[5], (down, west)),
            (turned_ref.at[1], tiles_out.at[6], (up, east)),
            (turned_ref.at[1], tiles_out.at[7], (down, east)),
        ]
    send_sem, recv_sem = sems
    return [
        remote(source, target, send_sem.at[i], recv_sem.at[i], peer)
        for i, (source, target, peer) in enumerate(plan)
    ]


def start_kernel(
    n_tile, n_obs, cap, control_ref, bg_hbm, spread_ref, holder_ref, anchor_ref, frac_ref,
    pos_ref, req_ref, rows_out, strips_out, corners_out, own_out, tiles_out, base_out,
    x_ref, y_ref, bg_ref, bg_sem, ask, asked, rows_acc, strips_acc, rows_b, strips_b, turned, rows_in, strips_in, corners_in,
    tiles_in, *sems,
):
    step = pl.program_id(0)
    _, rows_x, rows_y = control_ref.shape
    steps = base_out.shape[0] // CHUNK
    last = steps - 1
    swap_set, halo_set = sems[:3], sems[3:]

    @pl.when(step == 0)
    def _():
        greet_all(n_tile, n_obs)
        pltpu.make_async_copy(bg_hbm, bg_ref, bg_sem).start()
        request_kernel(cap, rows_y - 1, holder_ref, anchor_ref, frac_ref, ask, pos_ref)
        spread = spread_ref[...]
        square = jnp.concatenate([spread, jnp.zeros((rows_y - rows_x, rows_y), F32)], axis=0).T
        turned[0] = square[:8]
        turned[1] = square[rows_y - 8 :]
        strips_acc[...] = jnp.zeros_like(strips_acc)

    @pl.when(step == min(4, steps - 1))
    def _():
        await_all(n_tile, n_obs)
        swap_start(n_tile, n_obs, ask, asked, swap_set)

    lane = lax.broadcasted_iota(jnp.int32, (rows_x, LANES), 1)
    first = pl.multiple_of(step * CHUNK, CHUNK)
    for k, x in enumerate((0, 1, rows_x - 2, rows_x - 1)):
        rows_acc[k, pl.ds(first, CHUNK), :] = control_ref[:, x, :]
    held = [strips_acc[k] for k in range(4)]
    for i in range(CHUNK):
        level = step * CHUNK + i
        moved = pltpu.roll(control_ref[i], level, 1)
        for k, shift in enumerate((0, 1, rows_y - 1, rows_y - 2)):
            held[k] = jnp.where(lane == lax.rem(level + shift, LANES), moved, held[k])
    for k in range(4):
        strips_acc[k] = held[k]

    @pl.when(step == last)
    def _():
        rows_b[...] = rows_acc[...].astype(BF16)
        for k, shift in enumerate((0, LANES - 1, 1, 2)):
            strip = strips_acc[k] if shift == 0 else pltpu.roll(strips_acc[k], shift, 1)
            strips_b[k] = strip.astype(BF16)
            if k % 2 == 0:
                own_out[k // 2] = strip
        copies = halo_copies(
            n_tile, n_obs, (rows_b, strips_b, rows_in, strips_in, corners_in),
            (spread_ref, turned, tiles_in), halo_set,
        )
        for copy in copies:
            copy.start()
        swap_wait(n_tile, n_obs, ask, asked, swap_set)
        req_ref[...] = jnp.concatenate(
            [asked[p][:, :cap] for p in range(n_tile * n_obs)], axis=1
        )
        fill_weights(req_ref, rows_x, rows_y, x_ref, y_ref)
        pltpu.make_async_copy(bg_hbm, bg_ref, bg_sem).wait()

        def gather_base(chunk, _):
            first = pl.multiple_of(chunk * CHUNK, CHUNK)
            part = bg_ref[pl.ds(first, CHUNK)].reshape(CHUNK * rows_x, rows_y)
            gather_level(part, y_ref, x_ref, base_out, first)
            return 0

        lax.fori_loop(0, steps, gather_base, 0)
        for copy in copies:
            copy.wait()
        rows_out[...] = rows_in[...].astype(F32)
        strips_out[...] = strips_in[...].astype(F32)
        corners_out[...] = corners_in[...].astype(F32)
        tiles_out[...] = tiles_in[...]


def weight_fields(req, rows_x, rows_y):
    slots = req.shape[1]
    ax, ay = req[0:1].astype(jnp.int32), req[1:2].astype(jnp.int32)
    fx = req[2:3] + req[3:4] + req[4:5]
    fy = req[5:6] + req[6:7] + req[7:8]

    def ramp(size, place, frac):
        index = lax.broadcasted_iota(jnp.int32, (size, slots), 0)
        return jnp.where(index == place, 1.0 - frac, jnp.where(index == place + 1, frac, 0.0))

    return ramp(rows_x, ax, fx), ramp(rows_y, ay, fy)


def around(value, axis):
    size = value.shape[axis]
    return pltpu.roll(value, 1, axis) + pltpu.roll(value, size - 1, axis)


def strip_setup(adjoint, own_ref, strips_ref, corners_ref, tiles_ref, spread_ref):
    length, levels = own_ref.shape[1], own_ref.shape[2]
    index = lax.broadcasted_iota(jnp.int32, (8, levels), 0)

    def extended(base, low, high):
        return jnp.concatenate([base, jnp.where(index < 4, low, high)], axis=0)

    def plain(base):
        return jnp.concatenate([base, jnp.zeros((8, levels), F32)], axis=0)

    square = jnp.concatenate(
        [tiles_ref[t] for t in range(2, 8)] + [jnp.zeros((LANES - 48, LANES), F32)], axis=0
    ).T

    def coef(tile, row, first=0, size=length):
        at = 8 * (tile - 2) + row
        return jnp.broadcast_to(square[first : first + size, at : at + 1], (size, levels))

    def column(ref, at, size):
        return jnp.broadcast_to(ref[:, at : at + 1], (size, levels))

    size = spread_ref.shape[1]
    parts = []
    for side, (near, far, low, high, tile, rows, here, there) in enumerate(
        ((2, 3, 2, 3, 3, (7, 6), 0, 1), (0, 1, 0, 1, 2, (0, 1), size - 1, size - 2))
    ):
        s_near = extended(strips_ref[near], corners_ref[low, :8], corners_ref[high, 8:])
        s_far, s_own = plain(strips_ref[far]), plain(own_ref[side])
        d_near = extended(
            coef(tile, rows[0]),
            coef(4 + low, rows[0], 0, 8),
            coef(4 + high, rows[0], length - 8, 8),
        )
        d_here = extended(
            column(spread_ref, here, length),
            column(tiles_ref.at[0], here, 8),
            column(tiles_ref.at[1], here, 8),
        )
        if adjoint:
            d_far = plain(coef(tile, rows[1]))
            once = d_near * s_near
            first = s_near + around(once, 0) + d_far * s_far + d_here * s_own - 4.0 * once
            scaled = d_here * once
            parts += [once + around(scaled, 0) - 4.0 * scaled + d_near * first, scaled]
        else:
            first = s_near + d_near * (around(s_near, 0) + s_far + s_own - 4.0 * s_near)
            once = d_here * s_near
            parts += [
                once + d_here * (around(once, 0) - 4.0 * once + first),
                plain(column(spread_ref, there, length)) * once,
            ]
    return [part[:length] for part in parts]


PAD = 8


def fill_spread(spread_ref, tiles_ref, d_ref):
    rows_x = spread_ref.shape[0]
    d_ref[pl.ds(0, PAD), :] = tiles_ref[1]
    d_ref[pl.ds(PAD, rows_x), :] = spread_ref[...]
    d_ref[pl.ds(PAD + rows_x, PAD), :] = tiles_ref[0]


def rim_tiles(rows_ref, level, size):
    index = lax.broadcasted_iota(jnp.int32, (PAD, size), 0)

    def row(k):
        return jnp.broadcast_to(rows_ref[k, pl.ds(level, 1), :], (PAD, size))

    return jnp.where(index < 7, row(2), row(3)), jnp.where(index < 1, row(0), row(1))


def laplace(buf, i, first, count):
    centre = buf[i, pl.ds(first, count), :]
    size = centre.shape[1]
    lane = lax.broadcasted_iota(jnp.int32, centre.shape, 1)
    total = buf[i, pl.ds(first - 1, count), :] + buf[i, pl.ds(first + 1, count), :]
    total = total + jnp.where(lane == 0, 0.0, pltpu.roll(centre, 1, 1))
    total = total + jnp.where(lane == size - 1, 0.0, pltpu.roll(centre, size - 1, 1))
    return centre, total - 4.0 * centre


CHUNK = 8


def gather_level(block, y_ref, x_ref, out_ref, first):
    rows_x = x_ref.shape[0]
    got = jnp.dot(
        jnp.concatenate([block, block], axis=1), y_ref[...], preferred_element_type=F32
    )
    xs = x_ref[...]
    parts = [
        jnp.sum(got[i * rows_x : (i + 1) * rows_x] * xs, axis=0, keepdims=True)
        for i in range(CHUNK)
    ]
    out_ref[pl.ds(first, CHUNK), :] = jnp.concatenate(parts, axis=0)


def fill_weights(req_ref, rows_x, rows_y, x_ref, y_ref):
    xs, ys = weight_fields(req_ref[...], rows_x, rows_y)
    x_ref[...] = xs
    high, low = split_two(ys)
    y_ref[pl.ds(0, rows_y), :] = high
    y_ref[pl.ds(rows_y, rows_y), :] = low
    return xs, ys


def gather_kernel(
    n_tile, n_obs, cap, control_ref, base_ref, rows_ref, own_ref, strips_ref, corners_ref, tiles_ref,
    spread_ref, req_ref, got_ref, x_ref, y_ref, d_ref, fix_ref, delta_t, inc_ref, buf, buf_b,
    sent, got, *sems,
):
    step = pl.program_id(0)
    rows_x, rows_y = spread_ref.shape

    @pl.when(step == 0)
    def _():
        greet_all(n_tile, n_obs)
        xs, ys = fill_weights(req_ref, rows_x, rows_y, x_ref, y_ref)
        fill_spread(spread_ref, tiles_ref, d_ref)
        parts = strip_setup(False, own_ref, strips_ref, corners_ref, tiles_ref, spread_ref)
        rims = (0, 1, rows_y - 1, rows_y - 2)
        weights = jnp.concatenate([xs * ys[y : y + 1] for y in rims], axis=0)
        fix_ref[...] = lax.dot_general(
            weights.astype(BF16),
            jnp.concatenate(parts, axis=0).astype(BF16),
            (((0,), (0,)), ((), ())),
            preferred_element_type=F32,
        )

    wide = rows_x + PAD
    for i in range(CHUNK):
        level = step * CHUNK + i
        north, south = rim_tiles(rows_ref, level, rows_y)
        buf[i, pl.ds(0, PAD), :] = north
        buf[i, pl.ds(PAD, rows_x), :] = control_ref[i]
        buf[i, pl.ds(PAD + rows_x, PAD), :] = south
        centre, total = laplace(buf, i, PAD - 1, wide)
        buf_b[i, pl.ds(PAD - 1, wide), :] = centre + d_ref[pl.ds(PAD - 1, wide), :] * total
        centre, total = laplace(buf_b, i, PAD, rows_x)
        value = centre + d_ref[pl.ds(PAD, rows_x), :] * total
        inc_ref[pl.ds(i * rows_x, rows_x), :] = value.astype(BF16)
    first = pl.multiple_of(step * CHUNK, CHUNK)
    gather_level(inc_ref[...], y_ref, x_ref, delta_t, first)

    @pl.when(step == pl.num_programs(0) - 1)
    def _():
        base, delta = base_ref[...].T, delta_t[...].T + fix_ref[...]
        for p in range(n_tile * n_obs):
            here = slice(p * cap, (p + 1) * cap)
            sent[p] = jnp.concatenate([base[here], delta[here]], axis=0).astype(BF16)
        await_all(n_tile, n_obs)
        swap_start(n_tile, n_obs, sent, got, sems)
        swap_wait(n_tile, n_obs, sent, got, sems)
        got_ref[...] = got[...]


def radiance_kernel(
    n_tile, n_obs, cap, rows_x, rows_y, pos_ref, got_ref, innov_ref, var_ref, w1_ref, b1_ref, w2_ref,
    b2_ref, w3_ref, req_ref, dep_ref, grad_t_ref, rows_out, strips_out, corners_out, own_out,
    sent, back, rows_b, strips_b, rows_in, strips_in, corners_in, *sems,
):
    greet_all(n_tile, n_obs)
    owners = n_tile * n_obs
    count = pos_ref.shape[0]
    both = got_ref.shape[0]
    pos = pos_ref[...]
    peer = jnp.floor((pos.astype(F32) + 0.5) / cap).astype(jnp.int32)
    place = pos + peer * cap
    lane = lax.broadcasted_iota(jnp.int32, (count, both), 1)
    got = got_ref[...]
    pick_b = (lane == place).astype(F32).astype(BF16)
    pick_d = (lane == place + cap).astype(F32).astype(BF16)
    base = jnp.dot(pick_b, got, preferred_element_type=F32).astype(BF16)
    delta = jnp.dot(pick_d, got, preferred_element_type=F32).astype(BF16)

    def forward(a, b):
        return jnp.dot(a, b, preferred_element_type=F32)

    def backward(a, b):
        return lax.dot_general(a, b, (((1,), (1,)), ((), ())), preferred_element_type=F32)

    w1, w2, w3t = w1_ref[...], w2_ref[...], w3_ref[...]
    h_one = jnp.tanh(forward(base, w1) + b1_ref[...])
    d_one = 1.0 - h_one * h_one
    h_two = jnp.tanh(forward(h_one.astype(BF16), w2) + b2_ref[...])
    d_two = 1.0 - h_two * h_two
    t_one = (d_one * forward(delta, w1)).astype(BF16)
    t_two = (d_two * forward(t_one, w2)).astype(BF16)
    dep = (backward(t_two, w3t) - innov_ref[...].T) * var_ref[...]
    dep_ref[...] = dep.T
    s_two = (d_two * forward(dep.astype(BF16), w3t)).astype(BF16)
    s_one = (d_one * backward(s_two, w2)).astype(BF16)
    grad = backward(s_one, w1).astype(BF16)
    slots = owners * cap
    spots = lax.broadcasted_iota(jnp.int32, (count, slots), 1)
    pick = (spots == pos).astype(F32).astype(BF16)
    packed = lax.dot_general(pick, grad, (((0,), (0,)), ((), ())), preferred_element_type=F32)
    for p in range(owners):
        sent[p] = packed[p * cap : (p + 1) * cap].astype(BF16)
    await_all(n_tile, n_obs)
    swap_start(n_tile, n_obs, sent, back, sems[:3])
    xs, ys = weight_fields(req_ref[...], rows_x, rows_y)
    swap_wait(n_tile, n_obs, sent, back, sems[:3])

    grad_f = jnp.concatenate([back[p].astype(F32) for p in range(owners)], axis=0)
    grad = grad_f.astype(BF16)
    grad_t = grad_f.T
    grad_t_ref[...] = grad_t
    grad_tb = grad_t.astype(BF16)
    for k, y in enumerate((0, 1, rows_y - 1, rows_y - 2)):
        high, low = split_two(xs * ys[y : y + 1])
        strip = forward(high, grad) + forward(low, grad)
        strips_b[k] = strip.astype(BF16)
        if k % 2 == 0:
            own_out[k // 2] = strip
    for k, x in enumerate((0, 1, rows_x - 2, rows_x - 1)):
        high, low = split_two(ys * xs[x : x + 1])
        rows_b[k] = (backward(grad_tb, high) + backward(grad_tb, low)).astype(BF16)
    copies = halo_copies(
        n_tile, n_obs, (rows_b, strips_b, rows_in, strips_in, corners_in), None, sems[3:]
    )
    for copy in copies:
        copy.start()
    for copy in copies:
        copy.wait()
    rows_out[...] = rows_in[...].astype(F32)
    strips_out[...] = strips_in[...].astype(F32)
    corners_out[...] = corners_in[...].astype(F32)


def adjoint_kernel(
    control_ref, grad_t_ref, req_ref, rows_ref, own_ref, strips_ref, corners_ref,
    tiles_ref, spread_ref,
    out_ref, x_ref, y_ref, d_ref, fix_ref, lhs_ref, buf, buf_b, buf_f,
):
    step = pl.program_id(0)
    rows_x, rows_y = spread_ref.shape

    @pl.when(step == 0)
    def _():
        xs, ys = weight_fields(req_ref[...], rows_x, rows_y)
        x_ref[...] = xs
        high, low = split_two(ys.T)
        y_ref[:, pl.ds(0, rows_y)] = high
        y_ref[:, pl.ds(rows_y, rows_y)] = low
        fill_spread(spread_ref, tiles_ref, d_ref)
        parts = strip_setup(True, own_ref, strips_ref, corners_ref, tiles_ref, spread_ref)
        shifts = (0, 1, rows_y - 1, rows_y - 2)
        moved = [p if t == 0 else pltpu.roll(p, t, 1) for p, t in zip(parts, shifts)]
        lane = lax.broadcasted_iota(jnp.int32, (rows_x, rows_y), 1)
        for r in range(4):
            key = lax.rem(lane + (4 - r), 4)
            mixed = jnp.where(key == 0, moved[0], jnp.where(key == 1, moved[1], moved[3]))
            fix_ref[r] = jnp.where(key == 3, moved[2], mixed)

    xs = x_ref[...]
    for i in range(CHUNK):
        row = grad_t_ref[pl.ds(i, 1), :]
        lhs_ref[pl.ds(i * rows_x, rows_x), :] = (xs * row).astype(BF16)
    both = jnp.dot(lhs_ref[...], y_ref[...], preferred_element_type=F32)
    field = both[:, :rows_y] + both[:, rows_y:]
    wide = rows_x + PAD
    lane = lax.broadcasted_iota(jnp.int32, (rows_x, rows_y), 1)
    rim = (lane < 2) | (lane >= rows_y - 2)
    d_top, d_own, d_end = (
        d_ref[pl.ds(0, PAD), :], d_ref[pl.ds(PAD, rows_x), :], d_ref[pl.ds(PAD + rows_x, PAD), :],
    )
    for i in range(CHUNK):
        level = step * CHUNK + i
        north, south = rim_tiles(rows_ref, level, rows_y)
        own = field[i * rows_x : (i + 1) * rows_x]
        buf_f[i, pl.ds(0, PAD), :] = north
        buf_f[i, pl.ds(PAD, rows_x), :] = own
        buf_f[i, pl.ds(PAD + rows_x, PAD), :] = south
        buf[i, pl.ds(0, PAD), :] = d_top * north
        buf[i, pl.ds(PAD, rows_x), :] = d_own * own
        buf[i, pl.ds(PAD + rows_x, PAD), :] = d_end * south
        total = laplace(buf, i, PAD - 1, wide)[1]
        once = buf_f[i, pl.ds(PAD - 1, wide), :] + total
        buf_f[i, pl.ds(PAD - 1, wide), :] = once
        buf_b[i, pl.ds(PAD - 1, wide), :] = d_ref[pl.ds(PAD - 1, wide), :] * once
        total = laplace(buf_b, i, PAD, rows_x)[1]
        fix = pltpu.roll(fix_ref[i % 4], lax.rem(rows_y - level, rows_y), 1)
        value = buf_f[i, pl.ds(PAD, rows_x), :] + total + jnp.where(rim, fix, 0.0)
        out_ref[i] = control_ref[i] + value


def whole(array):
    rank = len(array.shape)
    return pl.BlockSpec(array.shape, lambda i: (0,) * rank, pipeline_mode=pl.Buffered(1))


def per_device(
    n_tile, n_obs, control, background, spread, obs_holder, obs_anchor, obs_frac, innovation,
    inverse_var, w_first, b_first, w_second, b_second, w_third,
):
    levels, rows_x, rows_y = control.shape
    owners = n_tile * n_obs
    count = obs_anchor.shape[0]
    channels = innovation.shape[1]
    cap = 3 * count // owners
    slots = owners * cap

    steps = levels // CHUNK
    block = pl.BlockSpec((CHUNK, rows_x, rows_y), lambda i: (i, 0, 0))
    shape = jax.ShapeDtypeStruct
    pair, strip = shape((2, rows_x, levels), F32), shape((4, rows_x, levels), F32)
    row, corner = shape((4, levels, rows_y), F32), shape((4, 16, levels), F32)
    tiles = shape((8, 8, LANES), F32)
    landing = [
        pltpu.VMEM(row.shape, BF16),
        pltpu.VMEM(strip.shape, BF16),
        pltpu.VMEM(row.shape, BF16),
        pltpu.VMEM(strip.shape, BF16),
        pltpu.VMEM(corner.shape, BF16),
    ]
    several = pltpu.SemaphoreType.DMA
    padded = pltpu.VMEM((CHUNK, rows_x + 2 * PAD, rows_y), F32)

    outs = (shape((count, 1), jnp.int32), shape((8, slots), F32), row, strip, corner, pair, tiles)
    outs += (shape((levels, slots), F32),)
    held = [spread, obs_holder, obs_anchor.reshape(1, count), obs_frac]
    pos, req, rows_c, strips_c, corners_c, own_c, tiles_c, base = pl.pallas_call(
        functools.partial(start_kernel, n_tile, n_obs, cap),
        grid=(steps,),
        out_shape=outs,
        in_specs=[block, pl.BlockSpec(memory_space=pl.ANY)] + [whole(a) for a in held],
        out_specs=tuple(whole(a) for a in outs),
        scratch_shapes=[
            pltpu.VMEM((rows_x, slots), F32),
            pltpu.VMEM((2 * rows_y, slots), BF16),
            pltpu.VMEM(background.shape, BF16),
            pltpu.SemaphoreType.DMA,
            pltpu.VMEM((owners, 8, LANES), F32),
            pltpu.VMEM((owners, 8, LANES), F32),
            pltpu.VMEM(row.shape, F32),
            pltpu.VMEM(strip.shape, F32),
            *landing[:2],
            pltpu.VMEM((2, 8, LANES), F32),
            *landing[2:],
            pltpu.VMEM(tiles.shape, F32),
            *swap_sems(owners),
            several((16,)),
            several((16,)),
        ],
        compiler_params=pltpu.CompilerParams(collective_id=0, has_side_effects=True),
        name="start",
    )(control, background, *held)

    held = [base, rows_c, own_c, strips_c, corners_c, tiles_c, spread, req]
    column = shape((owners, 2 * cap, levels), BF16)
    got = pl.pallas_call(
        functools.partial(gather_kernel, n_tile, n_obs, cap),
        grid=(steps,),
        out_shape=column,
        in_specs=[block] + [whole(a) for a in held],
        out_specs=whole(column),
        scratch_shapes=[
            pltpu.VMEM((rows_x, slots), F32),
            pltpu.VMEM((2 * rows_y, slots), BF16),
            pltpu.VMEM((rows_x + 2 * PAD, rows_y), F32),
            pltpu.VMEM((slots, levels), F32),
            pltpu.VMEM((levels, slots), F32),
            pltpu.VMEM((CHUNK * rows_x, rows_y), BF16),
            padded,
            padded,
            pltpu.VMEM(column.shape, BF16),
            pltpu.VMEM(column.shape, BF16),
            *swap_sems(owners),
        ],
        compiler_params=pltpu.CompilerParams(collective_id=1, has_side_effects=True),
        name="gather",
    )(control, *held)

    dep_t, grad_t, rows_a, strips_a, corners_a, own_a = pl.pallas_call(
        functools.partial(radiance_kernel, n_tile, n_obs, cap, rows_x, rows_y),
        out_shape=(
            shape((channels, count), F32), shape((levels, slots), F32), row, strip, corner, pair,
        ),
        in_specs=vmem(10),
        out_specs=tuple(vmem(6)),
        scratch_shapes=[
            pltpu.VMEM((owners, cap, levels), BF16),
            pltpu.VMEM((owners, cap, levels), BF16),
            *landing,
            *swap_sems(owners),
            several((8,)),
            several((8,)),
        ],
        compiler_params=pltpu.CompilerParams(collective_id=2, has_side_effects=True),
        name="radiances",
    )(
        pos, got.reshape(2 * slots, levels), innovation.T, inverse_var.reshape(1, -1), w_first,
        b_first.reshape(1, -1), w_second, b_second.reshape(1, -1), w_third.T, req,
    )

    held = [req, rows_a, own_a, strips_a, corners_a, tiles_c, spread]
    gradient = pl.pallas_call(
        adjoint_kernel,
        grid=(steps,),
        out_shape=jax.ShapeDtypeStruct(control.shape, F32),
        in_specs=[block, pl.BlockSpec((CHUNK, slots), lambda i: (i, 0))] + [whole(a) for a in held],
        out_specs=block,
        scratch_shapes=[
            pltpu.VMEM((rows_x, slots), F32),
            pltpu.VMEM((slots, 2 * rows_y), BF16),
            pltpu.VMEM((rows_x + 2 * PAD, rows_y), F32),
            pltpu.VMEM((4, rows_x, levels), F32),
            pltpu.VMEM((CHUNK * rows_x, slots), BF16),
            padded,
            padded,
            padded,
        ],
        name="adjoint",
    )(control, grad_t, *held)
    return (dep_t.T, gradient)


def solution(mesh):
    n_tile, n_obs = mesh.shape["tile"], mesh.shape["obs"]
    return jax.shard_map(
        functools.partial(per_device, n_tile, n_obs),
        mesh=mesh,
        in_specs=(
            P(None, "tile", "obs"),
            P(None, "tile", "obs"),
            P("tile", "obs"),
            P(("tile", "obs"), None),
            P(("tile", "obs")),
            P(None, ("tile", "obs")),
            P(("tile", "obs"), None),
            P(),
            P(),
            P(),
            P(),
            P(),
            P(),
        ),
        out_specs=(P(("tile", "obs"), None), P(None, "tile", "obs")),
        check_vma=False,
    )
```
